128 devices in a mesh: block: 8 (over y, core), node: 16 (over x, z).
Axes of the slice: x: 4, y: 4, z: 4, core: 2. Of those that a mesh axis runs over, the one named last changes fastest.
Arguments:
- vectors: float32 [8, 32768, 512], P('block', 'node'), may hold values from -6 to 6
- col_factors: float32 [8, 5, 512, 64, 128], P('block', None, 'node'), may hold values from -0.625 to 0.625
- row_factors: float32 [8, 4, 512, 64, 128], P('block', None, 'node'), may hold values from -0.625 to 0.625
- col_ranks: int32 [8, 5, 512], P('block', None, 'node'), may hold values from 16 to 64, as said below
- row_ranks: int32 [8, 4, 512], P('block', None, 'node'), may hold values from 16 to 64, as said below
- row_weights: float32 [32768], P('node'), may hold values from 0.05 to 0.5
Outputs:
- block_row: float32 [32768, 512], P('node')
- transposed: float32 [8, 32768, 512], P('block', 'node')
The draws below stay inside these ranges and needn't reach their ends.
Inputs may be any that keep to these rules, and one draw needn't show every extreme that they name: `col_ranks`: every rank is at least a quarter of 64; in each block and level the first span has rank 64. `row_ranks`: every rank is at least a quarter of 64; in each block and level the first span in row order has rank 64.
All inputs are finite; a program needn't handle non-finite values.
Results may differ from the reference program's by a relative error of at most 0.0001.
Values sent between devices are 32-bit elements; how exact they have to be, the bound alone decides.
No kernel may reach another device: no remote copies, remote signals or barrier semaphores. Data moves between devices by JAX's collectives and lax.ppermute only.
A program may use at most 128 MiB of HBM per device.

```python
import math
import jax
import jax.numpy as jnp
from jax import lax

VECS = 512
SPAN = 64
LOCAL_LEVELS = 5
NODE_LEVELS = 4
PER_PEER = 2
SPANS = 512
M = 32768
NBLK = 8
N_NODE = 16


def draw_col_ranks(key, part):
    table = jax.random.randint(key, (NBLK, LOCAL_LEVELS, SPANS), SPAN // 4, SPAN + 1)
    return table.at[:, :, 0].set(SPAN).astype(jnp.int32)


def draw_row_ranks(key, part):
    table = jax.random.randint(jax.random.fold_in(key, 7), (NBLK, NODE_LEVELS, SPANS), SPAN // 4, SPAN + 1)
    return table.at[:, :, 0].set(SPAN).astype(jnp.int32)


def block_scale(key, extent, pieces, low, largest):
    factor_of = 1.0
    for position, parts in pieces:
        heights = jax.random.uniform(jax.random.fold_in(jax.random.fold_in(key, 6), position), (parts,), jnp.float32, low / len(pieces), largest / len(pieces))
        factor_of = factor_of * jnp.repeat(jnp.exp(heights), extent[position] // parts).reshape((-1,) + (1,) * (len(extent) - 1 - position))
    return factor_of


def centred(rng, shape, scale, reach, cuts=(), kind=jnp.bfloat16):
    factor_of = block_scale(rng, shape, cuts, -0.22, 0.18) if cuts else 1.0
    drawn = jax.random.normal(rng, shape, jnp.float32) * scale * factor_of
    return jnp.minimum(jnp.maximum(drawn, -reach), reach).astype(kind)


def setup_inputs(seed: int = 0) -> dict:
    arg_keys = jax.random.split(jax.random.key(seed), 7)
    vectors = centred(arg_keys[0], (NBLK, M, VECS), 1.0, 6.0, ((0, 8), (1, 16)), jnp.float32)
    col_factors = centred(arg_keys[1], (NBLK, LOCAL_LEVELS, SPANS, SPAN, 2 * SPAN), (5 * SPAN // 4) ** -0.5, 0.625, ((0, 8), (2, 16)), jnp.float32)
    row_factors = centred(arg_keys[2], (NBLK, NODE_LEVELS, SPANS, SPAN, 2 * SPAN), (5 * SPAN // 4) ** -0.5, 0.625, ((0, 8), (2, 16)), jnp.float32)
    col_ranks = draw_col_ranks(jax.random.fold_in(arg_keys[6], 71), 0)
    row_ranks = draw_row_ranks(jax.random.fold_in(arg_keys[6], 71), 0)
    row_weights = jnp.clip(jnp.exp(math.log(0.5) - 2.3025851 * jax.random.uniform(arg_keys[5], (M,), jnp.float32) ** block_scale(arg_keys[5], (M,), ((0, 16),), -0.2, 0.2)), 0.05, 0.5)
    return {"vectors": vectors, "col_factors": col_factors, "row_factors": row_factors, "col_ranks": col_ranks, "row_ranks": row_ranks, "row_weights": row_weights}


def masked_factors(factors, rank_table):
    row_ids = jnp.arange(factors.shape[-2], dtype=jnp.int32)
    keep_rows = (row_ids[None, :] < rank_table[:, None]).astype(factors.dtype)
    return factors * keep_rows[:, :, None]


def apply_level(current, factors, bit_pos):
    span_count, rank_width, columns = current.shape
    stride = 2 ** bit_pos
    groups = span_count // (2 * stride)
    paired = current.reshape(groups, 2, stride, rank_width, columns)
    joined = jnp.concatenate([paired[:, 0], paired[:, 1]], axis=2)
    factor_blocks = factors.reshape(groups, 2, stride, rank_width, 2 * rank_width)
    result = jnp.einsum("atbkm,abmv->atbkv", factor_blocks, joined, precision=lax.Precision.HIGHEST)
    return result.reshape(span_count, rank_width, columns)


def apply_back(current, factors, bit_pos):
    span_count, rank_width, columns = current.shape
    stride = 2 ** bit_pos
    groups = span_count // (2 * stride)
    paired = current.reshape(groups, 2, stride, rank_width, columns)
    factor_blocks = factors.reshape(groups, 2, stride, rank_width, 2 * rank_width)
    joined = jnp.einsum("atbkm,atbkv->abmv", factor_blocks, paired, precision=lax.Precision.HIGHEST)
    result = jnp.stack([joined[:, :, :rank_width], joined[:, :, rank_width:]], axis=1)
    return result.reshape(span_count, rank_width, columns)


def swap_order(current):
    per_peer = PER_PEER
    shaped = current.reshape(N_NODE, N_NODE, per_peer, SPAN, current.shape[-1])
    return jnp.transpose(shaped, (1, 0, 2, 3, 4)).reshape(SPANS, SPAN, current.shape[-1])


def reference(vectors, col_factors, row_factors, col_ranks, row_ranks, row_weights):
    low_bits = LOCAL_LEVELS - NODE_LEVELS
    block_row = jnp.zeros((SPANS, SPAN, VECS), jnp.float32)
    for block_id in range(NBLK):
        current = vectors[block_id].reshape(SPANS, SPAN, VECS)
        for depth in range(LOCAL_LEVELS):
            current = apply_level(current, masked_factors(col_factors[block_id, depth], col_ranks[block_id, depth]), depth)
        current = swap_order(current)
        for depth in range(NODE_LEVELS):
            current = apply_level(current, masked_factors(row_factors[block_id, depth], row_ranks[block_id, depth]), low_bits + depth)
        block_row = block_row + current
    block_row = block_row.reshape(M, VECS)
    weighted = (row_weights[:, None] * block_row).reshape(SPANS, SPAN, VECS)
    outputs = []
    for block_id in range(NBLK):
        carried = weighted
        for depth in reversed(range(NODE_LEVELS)):
            carried = apply_back(carried, masked_factors(row_factors[block_id, depth], row_ranks[block_id, depth]), low_bits + depth)
        carried = swap_order(carried)
        for depth in reversed(range(LOCAL_LEVELS)):
            carried = apply_back(carried, masked_factors(col_factors[block_id, depth], col_ranks[block_id, depth]), depth)
        outputs.append(carried.reshape(M, VECS))
    return block_row, jnp.stack(outputs, axis=0)
```

```python
import functools
import jax
import jax.numpy as jnp
from jax import lax
from jax.experimental import pallas as pl
from jax.experimental.pallas import tpu as pltpu
from jax.sharding import PartitionSpec as P

CHUNKS = 2
F32 = jnp.float32


def split(value):
    high = value.astype(jnp.bfloat16)
    low = (value - high.astype(F32)).astype(jnp.bfloat16)
    return high, low


def pair_of(j, bit):
    first = ((j >> bit) << (bit + 1)) + (j & ((1 << bit) - 1))
    return first, first + (1 << bit)


def level_pass(load, store, f_ref, ranks, level, bit, back):
    span = f_ref.shape[-2]
    row_ids = lax.broadcasted_iota(jnp.int32, (span, 2 * span), 0)
    for j in range(f_ref.shape[-3] // 2):
        pair = pair_of(j, bit)
        factor = jnp.concatenate([jnp.where(row_ids < ranks[0, level, c], f_ref[0, c], 0.0) for c in pair], axis=0)
        if back:
            factor = factor.T
        f_high, f_low = split(factor)
        lhs = jnp.concatenate([f_high, f_low], axis=0)
        lhs = jnp.concatenate([lhs, lhs], axis=1)
        x_high, x_low = split(jnp.concatenate([load(c) for c in pair], axis=0))
        rhs = jnp.concatenate([x_high, x_low], axis=0)
        out = jnp.dot(lhs, rhs, preferred_element_type=F32)
        out = out[: 2 * span] + out[2 * span :]
        store(pair, out[:span], out[span:])


def reader(ref, span):
    return lambda c: ref[c * span : (c + 1) * span, :]


def writer(ref, span):
    def store(pair, first, second):
        for c, value in zip(pair, (first, second)):
            ref[c * span : (c + 1) * span, :] = value

    return store


def run_levels(levels, first_bit, back, ranks, f_ref, load, store, bufs):
    span = f_ref.shape[-2]
    for s in range(levels):
        level = levels - 1 - s if back else s
        src = load if s == 0 else reader(bufs[(s - 1) % 2], span)
        dst = store if s == levels - 1 else writer(bufs[s % 2], span)

        @pl.when(pl.program_id(0) == s)
        def _(src=src, dst=dst, level=level):
            level_pass(src, dst, f_ref, ranks, level, first_bit + level, back)


def cost(rows, columns, levels):
    return pl.CostEstimate(
        flops=levels * 16 * rows * 128 * columns, transcendentals=0, bytes_accessed=levels * (1 << 20) + 8 * rows * columns
    )


def factor_spec(factors, back):
    levels = factors.shape[1]
    return pl.BlockSpec((None, 1) + factors.shape[2:], lambda s: (0, levels - 1 - s if back else s, 0, 0, 0))


def whole(shape, chunk=0):
    return pl.BlockSpec(shape, lambda s: (0, chunk))


SMEM = pl.BlockSpec(memory_space=pltpu.SMEM)


def column_kernel(levels, back, ranks, x_ref, f_ref, *rest):
    o_ref, buf_a, buf_b = rest[-3:]
    span = f_ref.shape[-2]
    run_levels(levels, 0, back, ranks, f_ref, reader(x_ref, span), writer(o_ref, span), [buf_a, buf_b])


def column_tree(x, factors, ranks, columns, chunk):
    levels, rows = factors.shape[1], x.shape[0]
    return pl.pallas_call(
        functools.partial(column_kernel, levels, False),
        grid=(levels,),
        out_shape=jax.ShapeDtypeStruct((rows, columns), F32),
        in_specs=[SMEM, whole((rows, columns), chunk), factor_spec(factors, False)],
        out_specs=whole((rows, columns)),
        scratch_shapes=[pltpu.VMEM((rows, columns), F32)] * 2,
        cost_estimate=cost(rows, columns, levels),
        name="column_tree",
    )(ranks, x, factors)


def column_back(x, factors, ranks, into, chunk, total):
    levels = factors.shape[1]
    rows, columns = x.shape
    extra = [] if into is None else [into]
    return pl.pallas_call(
        functools.partial(column_kernel, levels, True),
        grid=(levels,),
        out_shape=jax.ShapeDtypeStruct((rows, total), F32),
        in_specs=[SMEM, whole((rows, columns)), factor_spec(factors, True)] + [pl.BlockSpec(memory_space=pl.ANY)] * len(extra),
        out_specs=whole((rows, columns), chunk),
        scratch_shapes=[pltpu.VMEM((rows, columns), F32)] * 2,
        input_output_aliases={3: 0} if extra else {},
        cost_estimate=cost(rows, columns, levels),
        name="column_back",
    )(ranks, x, factors, *extra)


def row_kernel(levels, first_bit, place, ranks, x_ref, f_ref, keep_ref, send_ref, buf_a, buf_b):
    span = f_ref.shape[-2]
    swap = place[1] == 1

    def store(pair, first, second):
        rows = slice(pair[0] * span, (pair[0] + 1) * span)
        keep_ref[rows, :] = jnp.where(swap, second, first)
        send_ref[rows, :] = jnp.where(swap, first, second)

    run_levels(levels, first_bit, False, ranks, f_ref, reader(x_ref, span), store, [buf_a, buf_b])


def row_tree(x, factors, ranks, place, first_bit):
    levels = factors.shape[1]
    rows, columns = x.shape
    half = jax.ShapeDtypeStruct((rows // 2, columns), F32)
    return pl.pallas_call(
        functools.partial(row_kernel, levels, first_bit),
        grid=(levels,),
        out_shape=(half, half),
        in_specs=[SMEM, SMEM, whole((rows, columns)), factor_spec(factors, False)],
        out_specs=(whole(half.shape), whole(half.shape)),
        scratch_shapes=[pltpu.VMEM((rows, columns), F32)] * 2,
        cost_estimate=cost(rows, columns, levels),
        name="row_tree",
    )(place, ranks, x, factors)


def add_halves_kernel(ring, place, keep_ref, got_ref, *outs):
    size = outs[0].shape[0]
    for d, out in enumerate(outs):
        rows = pl.ds(pl.multiple_of(lax.rem(place[0] + d, ring) * size, size), size)
        out[...] = keep_ref[rows, :] + got_ref[rows, :]


def add_halves(keep, got, place, ring):
    rows, columns = keep.shape
    piece = jax.ShapeDtypeStruct((rows // ring, columns), F32)
    return pl.pallas_call(
        functools.partial(add_halves_kernel, ring),
        grid=(1,),
        out_shape=(piece,) * ring,
        in_specs=[SMEM, whole(keep.shape), whole(keep.shape)],
        out_specs=(whole(piece.shape),) * ring,
        cost_estimate=pl.CostEstimate(flops=keep.size, transcendentals=0, bytes_accessed=12 * keep.size),
        name="add_halves",
    )(place, keep, got)


def add_pieces_kernel(*refs):
    total = refs[0][...]
    for ref in refs[1:-1]:
        total = total + ref[...]
    refs[-1][...] = total


def add_pieces(pieces):
    shape = pieces[0].shape
    return pl.pallas_call(
        add_pieces_kernel,
        grid=(1,),
        out_shape=jax.ShapeDtypeStruct(shape, F32),
        in_specs=[whole(shape)] * len(pieces),
        out_specs=whole(shape),
        cost_estimate=pl.CostEstimate(flops=4 * pieces[0].size, transcendentals=0, bytes_accessed=20 * pieces[0].size),
        name="add_pieces",
    )(*pieces)


def weigh_kernel(levels, first_bit, ring, has_into, place, ranks, *refs):
    pieces = refs[: 2 * ring]
    w_ref, f_ref = refs[2 * ring : 2 * ring + 2]
    b_ref, o_ref, buf_a, buf_b = refs[-4:]
    span = f_ref.shape[-2]
    size = pieces[0].shape[0]

    @pl.when(pl.program_id(0) == 0)
    def _():
        for n, piece in enumerate(pieces):
            side, d = divmod(n, ring)
            half = place[1] if side == 0 else 1 - place[1]
            start = half * (ring * size) + lax.rem(place[0] + ring - d, ring) * size
            rows = pl.ds(pl.multiple_of(start, size), size)
            value = piece[...]
            b_ref[rows, :] = value
            weight = w_ref[rows, :]
            weight = jnp.concatenate([weight] * (value.shape[1] // weight.shape[1]), axis=1)
            buf_b[rows, :] = value * weight

    run_levels(levels, first_bit, True, ranks, f_ref, reader(buf_b, span), writer(o_ref, span), [buf_a, buf_b])


def weigh_back(pieces, weights, factors, ranks, place, first_bit, into, chunk, total):
    levels = factors.shape[1]
    ring = len(pieces) // 2
    size, columns = pieces[0].shape
    rows = 2 * ring * size
    extra = [] if into is None else [into]
    return pl.pallas_call(
        functools.partial(weigh_kernel, levels, first_bit, ring, bool(extra)),
        grid=(levels,),
        out_shape=(jax.ShapeDtypeStruct((rows, total), F32), jax.ShapeDtypeStruct((rows, columns), F32)),
        in_specs=[SMEM, SMEM]
        + [whole(pieces[0].shape)] * len(pieces)
        + [whole(weights.shape), factor_spec(factors, True)]
        + [pl.BlockSpec(memory_space=pl.ANY)] * len(extra),
        out_specs=(whole((rows, columns), chunk), whole((rows, columns))),
        scratch_shapes=[pltpu.VMEM((rows, columns), F32)] * 2,
        input_output_aliases={4 + len(pieces): 0} if extra else {},
        cost_estimate=cost(rows, columns, levels),
        name="weigh_back",
    )(place, ranks, *pieces, weights, factors, *extra)


def exchange(x):
    nodes = lax.axis_size("node")
    rows, columns = x.shape
    out = lax.all_to_all(x.reshape(nodes, rows // nodes, columns), "node", split_axis=0, concat_axis=0, tiled=True)
    return out.reshape(rows, columns)


def shards(vectors, col_factors, row_factors, col_ranks, row_ranks, row_weights):
    rows, total = vectors.shape[1:]
    columns = total // CHUNKS
    low_bits = col_factors.shape[1] - row_factors.shape[1]
    ring = lax.axis_size("block") // 2
    sibling = [(b, b ^ 1) for b in range(2 * ring)]
    shift = [[(b, (b + 2 * d) % (2 * ring)) for b in range(2 * ring)] for d in range(ring)]
    index = lax.axis_index("block")
    place = jnp.stack([index // 2, index % 2]).astype(jnp.int32)
    flat = vectors.reshape(rows, total)
    weights = jnp.broadcast_to(row_weights[:, None], (rows, 128))
    chunks = range(CHUNKS)
    sent = [exchange(column_tree(flat, col_factors, col_ranks, columns, n)) for n in chunks]
    block_row = result = None
    back = []
    for n in chunks:
        keep, send = row_tree(sent[n], row_factors, row_ranks, place, low_bits)
        got = lax.ppermute(send, "block", sibling)
        pieces = add_halves(keep, got, place, ring)
        pieces = [pieces[0]] + [lax.ppermute(pieces[d], "block", shift[d]) for d in range(1, ring)]
        mine = add_pieces(pieces)
        mine = [mine] + [lax.ppermute(mine, "block", shift[d]) for d in range(1, ring)]
        theirs = [lax.ppermute(piece, "block", sibling) for piece in mine]
        block_row, t = weigh_back(mine + theirs, weights, row_factors, row_ranks, place, low_bits, block_row, n, total)
        back.append(exchange(t))
    for n in chunks:
        result = column_back(back[n], col_factors, col_ranks, result, n, total)
    return block_row, result.reshape(1, rows, total)


def solution(mesh):
    in_specs = (
        P("block", "node", None),
        P("block", None, "node", None, None),
        P("block", None, "node", None, None),
        P("block", None, "node"),
        P("block", None, "node"),
        P("node"),
    )
    out_specs = (P("node", None), P("block", "node", None))
    return jax.shard_map(shards, mesh=mesh, in_specs=in_specs, out_specs=out_specs, check_vma=False)
```

```python
import functools
import jax
import jax.numpy as jnp
from jax import lax
from jax.experimental import pallas as pl
from jax.experimental.pallas import tpu as pltpu
from jax.sharding import PartitionSpec as P


CHUNKS = 2
SUB = 2
F32 = jnp.float32
BF16 = jnp.bfloat16
PARAMS = pltpu.CompilerParams(vmem_limit_bytes=67043328)


def split(value):
    high = value.astype(jnp.bfloat16)
    low = (value - high.astype(F32)).astype(jnp.bfloat16)
    return high, low


def pair_of(j, bit):
    first = ((j >> bit) << (bit + 1)) + (j & ((1 << bit) - 1))
    return first, first + (1 << bit)


def level_pass(load, store, f_ref, ranks, level, bit, back):
    span = f_ref.shape[-2]
    row_ids = lax.broadcasted_iota(jnp.int32, (span, 2 * span), 0)
    for j in range(f_ref.shape[-3] // 2):
        pair = pair_of(j, bit)
        factor = jnp.concatenate([jnp.where(row_ids < ranks[level, 0, c], f_ref[0, c], 0.0) for c in pair], axis=0)
        if back:
            factor = factor.T
        f_high, f_low = split(factor)
        lhs = jnp.concatenate([f_high, f_low], axis=0)
        lhs = jnp.concatenate([lhs, lhs], axis=1)
        x_high, x_low = split(jnp.concatenate([load(c) for c in pair], axis=0))
        rhs = jnp.concatenate([x_high, x_low], axis=0)
        out = jnp.dot(lhs, rhs, preferred_element_type=F32)
        out = out[: 2 * span] + out[2 * span :]
        store(pair, out[:span], out[span:])


def reader(ref, span):
    return lambda c: ref[c * span : (c + 1) * span, :]


def writer(ref, span):
    def store(spans, *values):
        for c, value in zip(spans, values):
            ref[c * span : (c + 1) * span, :] = value

    return store


def run_levels(levels, first_bit, back, ranks, f_ref, load, store, bufs):
    span = f_ref.shape[-2]
    for s in range(levels):
        level = levels - 1 - s if back else s
        src = load if s == 0 else reader(bufs[(s - 1) % 2], span)
        dst = store if s == levels - 1 else writer(bufs[s % 2], span)

        @pl.when(pl.program_id(0) == s)
        def _(src=src, dst=dst, level=level):
            level_pass(src, dst, f_ref, ranks, level, first_bit + level, back)


def cost(rows, columns, levels):
    return pl.CostEstimate(
        flops=levels * 16 * rows * 128 * columns, transcendentals=0, bytes_accessed=levels * (1 << 20) + 8 * rows * columns
    )


def factor_spec(factors, back):
    levels = factors.shape[1]
    return pl.BlockSpec((None, 1) + factors.shape[2:], lambda s: (0, levels - 1 - s if back else s, 0, 0, 0))


def whole(shape, chunk=0):
    return pl.BlockSpec(shape, lambda s: (0, chunk))


SMEM = pl.BlockSpec(memory_space=pltpu.SMEM)


def column_kernel(levels, back, ranks, x_ref, f_ref, o_ref, buf_a, buf_b):
    span = f_ref.shape[-2]
    run_levels(levels, 0, back, ranks, f_ref, reader(x_ref, span), writer(o_ref, span), [buf_a, buf_b])


def column_tree(x, factors, ranks, columns, chunk):
    levels, rows = factors.shape[1], x.shape[0]
    return pl.pallas_call(
        functools.partial(column_kernel, levels, False),
        grid=(levels,),
        out_shape=jax.ShapeDtypeStruct((rows, columns), F32),
        in_specs=[SMEM, whole((rows, columns), chunk), factor_spec(factors, False)],
        out_specs=whole((rows, columns)),
        scratch_shapes=[pltpu.VMEM((rows, columns), F32)] * 2,
        compiler_params=PARAMS,
        cost_estimate=cost(rows, columns, levels),
        name="column_tree",
    )(ranks, x, factors)


def quad_of(j, bit):
    base = ((j >> bit) << (bit + 2)) + (j & ((1 << bit) - 1))
    return [base + (n << bit) for n in range(4)]


def three(high, low, axis):
    return jnp.concatenate([high, high, low] if axis == 1 else [high, low, high], axis=axis)


def merge_kernel(first_bit, ranks, fa_ref, fb_ref, *refs):
    g_ref, t_ref = refs[-2:]
    span = fa_ref.shape[-2]
    lane = lax.broadcasted_iota(jnp.int32, (2 * span, 2 * span), 1)
    row_ids = lax.broadcasted_iota(jnp.int32, (span, 2 * span), 0)
    for s in range(2):

        @pl.when(pl.program_id(0) == s)
        def _(s=s):
            bit = first_bit + 2 * s
            masked = lambda ref, level, c: jnp.where(row_ids < ranks[level, 0, c], ref[0, c], 0.0)
            for j in range(g_ref.shape[1]):
                quad = quad_of(j, bit)
                rows = [None] * 4
                for a in range(2):
                    spans = (quad[a], quad[2 + a])
                    inner = jnp.concatenate([masked(fa_ref, 2 * s, c) for c in spans], axis=0)
                    outer = jnp.concatenate([masked(fb_ref, 2 * s + 1, c) for c in spans], axis=0)
                    outer = jnp.concatenate([jnp.where(lane < span, outer, 0.0), jnp.where(lane < span, 0.0, outer)], axis=0)
                    both = jnp.dot(three(*split(outer), 1), three(*split(inner), 0), preferred_element_type=F32)
                    both = jnp.concatenate([both[: 2 * span], both[2 * span :]], axis=1)
                    rows[a], rows[2 + a] = both[:span], both[span:]
                merged = jnp.concatenate(rows, axis=0)
                for out, value in ((g_ref, merged), (t_ref, merged.T)):
                    high, low = split(value)
                    out[0, j, 0] = high
                    out[0, j, 1] = low


def merge_columns_kernel(first_bit, last, ranks, fa_ref, fb_ref, fe_ref, w_ref, v_ref, g_ref, t_ref):
    span = fa_ref.shape[-2]
    row_ids = lax.broadcasted_iota(jnp.int32, (span, 2 * span), 0)

    @pl.when(pl.program_id(0) == 0)
    def _():
        for j in range(w_ref.shape[0]):
            pair = pair_of(j, last)
            factor = jnp.concatenate([jnp.where(row_ids < ranks[last, 0, c], fe_ref[0, c], 0.0) for c in pair], axis=0)
            w_ref[j] = jnp.concatenate(split(factor), axis=0)
            v_ref[j] = jnp.concatenate(split(factor.T), axis=0)

    merge_kernel(first_bit, ranks, fa_ref, fb_ref, g_ref, t_ref)


def merge_rows_kernel(first_bit, ranks, fa_ref, fb_ref, weight_ref, b_ref, g_ref, t_ref):
    @pl.when(pl.program_id(0) == 0)
    def _():
        size = weight_ref.shape[1]
        for n in range(weight_ref.shape[0]):
            b_ref[n * size : (n + 1) * size, :] = jnp.broadcast_to(weight_ref[n : n + 1, :], (size, size)).T

    merge_kernel(first_bit, ranks, fa_ref, fb_ref, g_ref, t_ref)


def level_spec(factors, index):
    return pl.BlockSpec((None, 1) + factors.shape[2:], lambda s: (0, index(s), 0, 0, 0))


def merged_shapes(factors):
    quads, side = factors.shape[2] // 4, 4 * factors.shape[3]
    shape = jax.ShapeDtypeStruct((2, quads, 2, side, side), BF16)
    return shape, pl.BlockSpec((1, quads, 2, side, side), lambda s: (s, 0, 0, 0, 0))


def merge_columns(factors, ranks):
    shape, spec = merged_shapes(factors)
    last = factors.shape[1] - 1
    pairs, width = factors.shape[2] // 2, 2 * factors.shape[3]
    single = jax.ShapeDtypeStruct((pairs, 2 * width, width), BF16)
    single_spec = pl.BlockSpec(single.shape, lambda s: (0, 0, 0))
    return pl.pallas_call(
        functools.partial(merge_columns_kernel, 0, last),
        grid=(2,),
        out_shape=(single, single, shape, shape),
        in_specs=[SMEM]
        + [level_spec(factors, f) for f in (lambda s: 2 * s, lambda s: 2 * s + 1, lambda s: last)],
        out_specs=(single_spec, single_spec, spec, spec),
        compiler_params=PARAMS,
        cost_estimate=pl.CostEstimate(flops=10**10, transcendentals=0, bytes_accessed=15 << 20),
        name="merge_columns",
    )(ranks, factors, factors, factors)


def merge_rows(factors, ranks, weights, first_bit):
    shape, spec = merged_shapes(factors)
    weights = weights.reshape(-1, 128)
    rows = weights.size
    return pl.pallas_call(
        functools.partial(merge_rows_kernel, first_bit),
        grid=(2,),
        out_shape=(jax.ShapeDtypeStruct((rows, 128), F32), shape, shape),
        in_specs=[SMEM] + [level_spec(factors, f) for f in (lambda s: 2 * s, lambda s: 2 * s + 1)] + [whole2(weights.shape)],
        out_specs=(whole2((rows, 128)), spec, spec),
        compiler_params=PARAMS,
        cost_estimate=pl.CostEstimate(flops=10**10, transcendentals=0, bytes_accessed=12 << 20),
        name="merge_rows",
    )(ranks, factors, factors, weights)


def whole2(shape):
    return pl.BlockSpec(shape, lambda s: (0, 0))


def spans_of(ref, span, bit, sub, streamed):
    def rows(q, n, count):
        if streamed and len(ref.shape) == 4:
            return (n, 0, slice(q * span, (q + 1) * span), slice(None))
        group = quad_of if count == 4 else pair_of
        if streamed:
            c = group(q, bit)[n]
            return (slice(c * span, (c + 1) * span), slice(None))
        total = ref.shape[0] // span // count // SUB
        return (pl.ds(pl.multiple_of(group(sub * total + q, bit)[n] * span, span), span), slice(None))

    def load(q, count):
        return jnp.concatenate([ref[rows(q, n, count)] for n in range(count)], axis=0)

    def store(q, values):
        for n, value in enumerate(values):
            ref[rows(q, n, len(values))] = value

    return load, store


def quad_pass(load, store, g_ref):
    for q in range(g_ref.shape[0]):
        x = load(q, 4)
        out = jnp.dot(three(g_ref[q, 0], g_ref[q, 1], 1), three(*split(x), 0), preferred_element_type=F32)
        size = out.shape[0] // 4
        store(q, [out[n * size : (n + 1) * size] for n in range(4)])


def pair_pass(load, store, w_ref):
    for q in range(w_ref.shape[0]):
        x = load(q, 2)
        lhs = jnp.concatenate([w_ref[q], w_ref[q]], axis=1)
        out = jnp.dot(lhs, jnp.concatenate(split(x), axis=0), preferred_element_type=F32)
        size = out.shape[0] // 4
        out = out[: 2 * size] + out[2 * size :]
        store(q, [out[:size], out[size:]])


def run_stages(stages, x_ref, o_ref, bufs, span):
    for s, (bit, stage) in enumerate(stages):
        first, last = s == 0, s == len(stages) - 1

        @pl.when(pl.program_id(0) // SUB == s)
        def _(s=s, bit=bit, stage=stage, first=first, last=last):
            sub = lax.rem(pl.program_id(0), SUB)
            if callable(x_ref) and first:
                load = x_ref(sub, bit)
            else:
                load = spans_of(x_ref if first else bufs[(s - 1) % 2], span, bit, sub, first)[0]
            if callable(o_ref) and last:
                store = o_ref
            else:
                store = spans_of(o_ref if last else bufs[s % 2], span, bit, sub, last)[1]
            stage(load, store)


def part(step, stage):
    return jnp.clip(step - stage * SUB, 0, SUB - 1)


def merged_spec(merged, first, back):
    quads = merged.shape[1] // SUB

    def index(step):
        at = jnp.clip(step - first * SUB, 0, 2 * SUB - 1)
        stage = at // SUB
        return (1 - stage if back else stage, lax.rem(at, SUB), 0, 0, 0)

    return pl.BlockSpec((None, quads) + merged.shape[2:], index)


def merged_column_kernel(back, last, x_ref, w_ref, g_ref, *rest):
    o_ref, buf_a, buf_b = rest[-3:]
    span = w_ref.shape[-1] // 2
    quads = lambda load, store: quad_pass(load, store, g_ref)
    stages = [(0, quads), (2, quads), (last, lambda load, store: pair_pass(load, store, w_ref))]
    run_stages(stages[::-1] if back else stages, x_ref, o_ref, [buf_a, buf_b], span)


def merged_columns(x, single, merged, back, columns, chunk=0, into=None, out_chunk=0, total=None, after=()):
    rows = x.shape[0]
    extra = list(after) if into is None else [into] + list(after)
    size = single.shape[0] // SUB * 64
    w_spec = pl.BlockSpec((size // 64,) + single.shape[1:], lambda s: (part(s, 0 if back else 2), 0, 0))
    if back:
        x = x.reshape(2, SUB, size, columns)
        x_spec = pl.BlockSpec((2, 1, size, columns), lambda s: (0, part(s, 0), 0, 0))
        out_shape = (rows, total)
        o_spec = pl.BlockSpec((rows // SUB, columns), lambda s: (part(s, 2), out_chunk))
    else:
        x_spec = pl.BlockSpec((rows // SUB, columns), lambda s: (part(s, 0), chunk))
        out_shape = (2, SUB, size, columns)
        o_spec = pl.BlockSpec((2, 1, size, columns), lambda s: (0, part(s, 2), 0, 0))
    out = pl.pallas_call(
        functools.partial(merged_column_kernel, back, 4),
        grid=(3 * SUB,),
        out_shape=jax.ShapeDtypeStruct(out_shape, F32),
        in_specs=[x_spec, w_spec, merged_spec(merged, 1 if back else 0, back)] + [pl.BlockSpec(memory_space=pl.ANY)] * len(extra),
        out_specs=o_spec,
        scratch_shapes=[pltpu.VMEM((rows, columns), F32)] * 2,
        input_output_aliases={} if into is None else {3: 0},
        compiler_params=PARAMS,
        cost_estimate=pl.CostEstimate(flops=4 * 10**9, transcendentals=0, bytes_accessed=9 << 20),
        name="column_back" if back else "column_tree_merged",
    )(x, single, merged, *extra)
    return out if back else out.reshape(rows, columns)


def row_kernel(first_bit, span, place, x_ref, g_ref, keep_ref, send_ref, buf):
    swap = place[1] == 1

    def store(q, values):
        at = slice(q * span, (q + 1) * span)
        for n in range(2):
            keep_ref[n, 0, at, :] = jnp.where(swap, values[n + 2], values[n])
            send_ref[n, 0, at, :] = jnp.where(swap, values[n], values[n + 2])

    quads = lambda load, put: quad_pass(load, put, g_ref)
    run_stages([(first_bit, quads), (first_bit + 2, quads)], x_ref, store, [buf], span)


def row_tree(x, merged, place, first_bit, span):
    rows, columns = x.shape
    size = rows // 4 // SUB
    half = jax.ShapeDtypeStruct((2, SUB, size, columns), F32)
    half_spec = pl.BlockSpec((2, 1, size, columns), lambda s: (0, part(s, 1), 0, 0))
    keep, send = pl.pallas_call(
        functools.partial(row_kernel, first_bit, span),
        grid=(2 * SUB,),
        out_shape=(half, half),
        in_specs=[SMEM, pl.BlockSpec((rows // SUB, columns), lambda s: (part(s, 0), 0)), merged_spec(merged, 0, False)],
        out_specs=(half_spec, half_spec),
        scratch_shapes=[pltpu.VMEM((rows, columns), F32)],
        compiler_params=PARAMS,
        cost_estimate=pl.CostEstimate(flops=3 * 10**9, transcendentals=0, bytes_accessed=8 << 20),
        name="row_tree",
    )(place, x, merged)
    return keep.reshape(rows // 2, columns), send.reshape(rows // 2, columns)


def add_halves_kernel(ring, place, keep_ref, got_ref, *refs):
    outs, (k_buf, g_buf, in_sems, out_sems) = refs[:ring], refs[ring:]
    size = outs[0].shape[0]
    copies = []
    for d in range(ring):
        rows = pl.ds(pl.multiple_of(lax.rem(place[0] + d, ring) * size, size), size)
        copies.append(pltpu.make_async_copy(keep_ref.at[rows], k_buf.at[d], in_sems.at[0, d]))
        copies.append(pltpu.make_async_copy(got_ref.at[rows], g_buf.at[d], in_sems.at[1, d]))
    for copy in copies:
        copy.start()
    sends = []
    for d, out in enumerate(outs):
        copies[2 * d].wait()
        copies[2 * d + 1].wait()
        g_buf[d] = g_buf[d] + k_buf[d]
        sends.append(pltpu.make_async_copy(g_buf.at[d], out, out_sems.at[d]))
        sends[-1].start()
    for send in sends:
        send.wait()


HBM = pl.BlockSpec(memory_space=pltpu.HBM)


def add_halves(keep, got, place, ring):
    rows, columns = keep.shape
    size = rows // ring
    piece = jax.ShapeDtypeStruct((size, columns), F32)
    return pl.pallas_call(
        functools.partial(add_halves_kernel, ring),
        out_shape=(piece,) * ring,
        in_specs=[SMEM0, HBM, HBM],
        out_specs=(HBM,) * ring,
        scratch_shapes=[pltpu.VMEM((ring, size, columns), F32)] * 2
        + [pltpu.SemaphoreType.DMA((2, ring)), pltpu.SemaphoreType.DMA((ring,))],
        compiler_params=PARAMS,
        cost_estimate=pl.CostEstimate(flops=keep.size, transcendentals=0, bytes_accessed=12 * keep.size),
        name="add_halves",
    )(place, keep, got)


SMEM0 = pl.BlockSpec(memory_space=pltpu.SMEM)


def add_pieces_kernel(count, *refs):
    pieces, out = refs[:count], refs[count]
    buf, in_sems, out_sems = refs[count + 1 :]
    parts = buf.shape[1]
    size = out.shape[0] // parts
    copies = []
    for p in range(parts):
        for n, piece in enumerate(pieces):
            copies.append(pltpu.make_async_copy(piece.at[pl.ds(p * size, size)], buf.at[n, p], in_sems.at[n, p]))
            copies[-1].start()
    sends = []
    for p in range(parts):
        for n in range(count):
            copies[p * count + n].wait()
        total = buf[0, p]
        for n in range(1, count):
            total = total + buf[n, p]
        buf[0, p] = total
        sends.append(pltpu.make_async_copy(buf.at[0, p], out.at[pl.ds(p * size, size)], out_sems.at[p]))
        sends[-1].start()
    for send in sends:
        send.wait()


def add_pieces(pieces):
    rows, columns = pieces[0].shape
    count, parts = len(pieces), 2
    return pl.pallas_call(
        functools.partial(add_pieces_kernel, count),
        out_shape=jax.ShapeDtypeStruct((rows, columns), F32),
        in_specs=[HBM] * count,
        out_specs=HBM,
        scratch_shapes=[pltpu.VMEM((count, parts, rows // parts, columns), F32)]
        + [pltpu.SemaphoreType.DMA((count, parts)), pltpu.SemaphoreType.DMA((parts,))],
        compiler_params=PARAMS,
        cost_estimate=pl.CostEstimate(flops=4 * pieces[0].size, transcendentals=0, bytes_accessed=20 * pieces[0].size),
        name="add_pieces",
    )(*pieces)


def weigh_kernel(first_bit, span, ring, chunk, place, *refs):
    pieces = refs[: 2 * ring]
    w_ref, g_ref = refs[2 * ring : 2 * ring + 2]
    b_ref, o_ref, x_buf, buf, in_sems, out_sem = refs[-6:]
    size, columns = pieces[0].shape
    step = pl.program_id(0)
    out_copy = pltpu.make_async_copy(x_buf, b_ref.at[:, pl.ds(chunk * columns, columns)], out_sem)

    @pl.when(step == 0)
    def _():
        copies = []
        for n, piece in enumerate(pieces):
            side, d = divmod(n, ring)
            half = place[1] if side == 0 else 1 - place[1]
            start = half * (ring * size) + lax.rem(place[0] + ring - d, ring) * size
            rows = pl.ds(pl.multiple_of(start, size), size)
            copies.append(pltpu.make_async_copy(piece, x_buf.at[rows], in_sems.at[n]))
            copies[-1].start()
        for copy in copies:
            copy.wait()
        out_copy.start()

    def weighted(sub, bit):
        load, _ = spans_of(x_buf, span, bit, sub, False)
        load_weight, _ = spans_of(w_ref, span, bit, sub, False)

        def read(q, count):
            value, weight = load(q, count), load_weight(q, count)
            return value * jnp.concatenate([weight] * (value.shape[1] // weight.shape[1]), axis=1)

        return read

    quads = lambda load, store: quad_pass(load, store, g_ref)
    run_stages([(first_bit + 2, quads), (first_bit, quads)], weighted, o_ref, [buf], span)

    @pl.when(step == pl.num_programs(0) - 1)
    def _():
        out_copy.wait()


def weigh_back(pieces, weights, merged, place, first_bit, span, into, chunk, total, after=()):
    ring = len(pieces) // 2
    size, columns = pieces[0].shape
    rows = 2 * ring * size
    extra = list(after) if into is None else [into] + list(after)
    hbm = pl.BlockSpec(memory_space=pltpu.HBM)
    return pl.pallas_call(
        functools.partial(weigh_kernel, first_bit, span, ring, chunk),
        grid=(2 * SUB,),
        out_shape=(jax.ShapeDtypeStruct((rows, total), F32), jax.ShapeDtypeStruct((rows, columns), F32)),
        in_specs=[SMEM]
        + [hbm] * len(pieces)
        + [whole(weights.shape), merged_spec(merged, 0, True)]
        + [pl.BlockSpec(memory_space=pl.ANY)] * len(extra),
        out_specs=(hbm, pl.BlockSpec((rows // SUB, columns), lambda s: (part(s, 1), 0))),
        scratch_shapes=[pltpu.VMEM((rows, columns), F32)] * 2
        + [pltpu.SemaphoreType.DMA((len(pieces),)), pltpu.SemaphoreType.DMA],
        input_output_aliases={} if into is None else {3 + len(pieces): 0},
        compiler_params=PARAMS,
        cost_estimate=pl.CostEstimate(flops=3 * 10**9, transcendentals=0, bytes_accessed=12 << 20),
        name="weigh_back",
    )(place, *pieces, weights, merged, *extra)


def exchange(x):
    nodes = lax.axis_size("node")
    rows, columns = x.shape
    out = lax.all_to_all(x.reshape(nodes, rows // nodes, columns), "node", split_axis=0, concat_axis=0, tiled=True)
    return out.reshape(rows, columns)


def shards(vectors, col_factors, row_factors, col_ranks, row_ranks, row_weights):
    rows, total = vectors.shape[1:]
    columns = total // CHUNKS
    low_bits = col_factors.shape[1] - row_factors.shape[1]
    ring = lax.axis_size("block") // 2
    sibling = [(b, b ^ 1) for b in range(2 * ring)]
    shift = [[(b, (b + 2 * d) % (2 * ring)) for b in range(2 * ring)] for d in range(ring)]
    index = lax.axis_index("block")
    place = jnp.stack([index // 2, index % 2]).astype(jnp.int32)
    span = col_factors.shape[3]
    flat = vectors.reshape(rows, total)
    col_ranks = jnp.transpose(col_ranks, (1, 0, 2))
    row_ranks = jnp.transpose(row_ranks, (1, 0, 2))
    chunks = range(CHUNKS)
    t = column_tree(flat, col_factors, col_ranks, columns, 0)
    sent = [exchange(t)]
    single, single_back, col_merged, col_back = merge_columns(col_factors, col_ranks)
    weights, row_merged, row_back = merge_rows(row_factors, row_ranks, row_weights, low_bits)
    for n in chunks[1:]:
        t = merged_columns(flat, single, col_merged, False, columns, n, after=[weights])
        sent.append(exchange(t))
    halves = []
    for n in chunks:
        halves.append(row_tree(sent[n], row_merged, place, low_bits, span))

    def start(n):
        got = lax.ppermute(halves[n][1], "block", sibling)
        return add_halves(halves[n][0], got, place, ring)

    block_row = result = None
    back = []
    pieces = start(0)
    for n in chunks:
        later = n + 1 < CHUNKS
        got = [pieces[0]]
        for d in range(1, ring):
            got.append(lax.ppermute(pieces[d], "block", shift[d]))
        total_piece = add_pieces(got)
        mine = [total_piece]
        for d in range(1, ring):
            mine.append(lax.ppermute(total_piece, "block", shift[d]))
        if later:
            pieces = start(n + 1)
            mine[1:], pieces = lax.optimization_barrier((mine[1:], pieces))
        theirs = [lax.ppermute(piece, "block", sibling) for piece in mine]
        block_row, t = weigh_back(mine + theirs, weights, row_back, place, low_bits, span, block_row, n, total)
        back.append(exchange(t))
    for n in chunks:
        result = merged_columns(back[n], single_back, col_back, True, columns, 0, result, n, total)
    return block_row, result.reshape(1, rows, total)


def solution(mesh):
    in_specs = (
        P("block", "node", None),
        P("block", None, "node", None, None),
        P("block", None, "node", None, None),
        P("block", None, "node"),
        P("block", None, "node"),
        P("node"),
    )
    out_specs = (P("node", None), P("block", "node", None))
    return jax.shard_map(shards, mesh=mesh, in_specs=in_specs, out_specs=out_specs, check_vma=False)
```

```python
import functools
import jax
import jax.numpy as jnp
from jax import lax
from jax.experimental import pallas as pl
from jax.experimental.pallas import tpu as pltpu
from jax.sharding import PartitionSpec as P


CHUNKS = 2
F32 = jnp.float32
BF16 = jnp.bfloat16
PARAMS = pltpu.CompilerParams(vmem_limit_bytes=67043328)


def split(value):
    high = value.astype(jnp.bfloat16)
    low = (value - high.astype(F32)).astype(jnp.bfloat16)
    return high, low


def pair_of(j, bit):
    first = ((j >> bit) << (bit + 1)) + (j & ((1 << bit) - 1))
    return first, first + (1 << bit)


PARTS = 4


def rows_of(c, span):
    return slice(c * span, (c + 1) * span)


def take(ref, spans, span):
    return jnp.concatenate([ref[rows_of(c, span), :] for c in spans], axis=0)


def put(ref, spans, span, value):
    for n, c in enumerate(spans):
        ref[rows_of(c, span), :] = value[n * span : (n + 1) * span]


class Copies:
    def __init__(self, sems):
        self.sems, self.used = sems, 0

    def start(self, source, target):
        copy = pltpu.make_async_copy(source, target, self.sems.at[self.used])
        self.used += 1
        copy.start()
        return copy


def wait_all(copies):
    for copy in copies:
        copy.wait()


def part_rows(rows, halves):
    size = rows // PARTS // halves
    return [[pl.ds(h * (rows // halves) + p * size, size) for h in range(halves)] for p in range(PARTS)]


def pair_product(f_high, f_low, x):
    lhs = jnp.concatenate([f_high, f_low], axis=0)
    lhs = jnp.concatenate([lhs, lhs], axis=1)
    out = jnp.dot(lhs, jnp.concatenate(split(x), axis=0), preferred_element_type=F32)
    half = out.shape[0] // 2
    return out[:half] + out[half:]


def column_kernel(chunk, ranks, x_ref, f_ref, o_ref, x_buf, f_buf, buf_a, buf_b, o_buf, sems):
    levels, count, span = f_buf.shape[:3]
    rows, columns = x_buf.shape
    copies = Copies(sems)
    at = pl.ds(chunk * columns, columns)
    first = []
    size = count // PARTS
    for p in range(PARTS):
        first.append(
            [
                copies.start(f_ref.at[0, 0, pl.ds(p * size, size)], f_buf.at[0, pl.ds(p * size, size)]),
                copies.start(x_ref.at[pl.ds(p * size * span, size * span), at], x_buf.at[pl.ds(p * size * span, size * span)]),
            ]
        )
    later = [copies.start(f_ref.at[0, level], f_buf.at[level]) for level in range(1, levels)]
    bufs = [x_buf] + [(buf_a, buf_b)[level % 2] for level in range(levels - 1)] + [o_buf]
    row_ids = lax.broadcasted_iota(jnp.int32, (span, 2 * span), 0)
    outs = []
    for level in range(levels):
        if level:
            later[level - 1].wait()
        for p in range(PARTS):
            if level == 0:
                wait_all(first[p])
            for j in range(p * size // 2, (p + 1) * size // 2):
                pair = pair_of(j, level)
                factor = jnp.concatenate(
                    [jnp.where(row_ids < ranks[level, 0, c], f_buf[level, c], 0.0) for c in pair], axis=0
                )
                put(bufs[level + 1], pair, span, pair_product(*split(factor), take(bufs[level], pair, span)))
            if level == levels - 1:
                outs += [copies.start(o_buf.at[at], o_ref.at[at]) for at in part_rows(rows, 2)[p]]
    wait_all(outs)


def column_tree(x, factors, ranks, columns, chunk):
    rows = x.shape[0]
    return pl.pallas_call(
        functools.partial(column_kernel, chunk),
        out_shape=jax.ShapeDtypeStruct((rows, columns), F32),
        in_specs=[SMEM0, HBM, HBM],
        out_specs=HBM,
        scratch_shapes=[pltpu.VMEM((rows, columns), F32), pltpu.VMEM(factors.shape[1:], F32)]
        + [pltpu.VMEM((rows, columns), F32)] * 3
        + [pltpu.SemaphoreType.DMA((32,))],
        compiler_params=PARAMS,
        cost_estimate=pl.CostEstimate(flops=5 * 10**9, transcendentals=0, bytes_accessed=9 << 20),
        name="column_tree",
    )(ranks, x, factors)


SMEM0 = pl.BlockSpec(memory_space=pltpu.SMEM)
HBM = pl.BlockSpec(memory_space=pltpu.HBM)
SMEM = SMEM0


def quad_of(j, bit):
    base = ((j >> bit) << (bit + 2)) + (j & ((1 << bit) - 1))
    return [base + (n << bit) for n in range(4)]


def three(high, low, axis):
    return jnp.concatenate([high, high, low] if axis == 1 else [high, low, high], axis=axis)


def merge_kernel(first_bit, ranks, fa_ref, fb_ref, *refs):
    g_ref, t_ref = refs[-2:]
    span = fa_ref.shape[-2]
    lane = lax.broadcasted_iota(jnp.int32, (2 * span, 2 * span), 1)
    row_ids = lax.broadcasted_iota(jnp.int32, (span, 2 * span), 0)
    for s in range(2):

        @pl.when(pl.program_id(0) == s)
        def _(s=s):
            bit = first_bit + 2 * s
            masked = lambda ref, level, c: jnp.where(row_ids < ranks[level, 0, c], ref[0, c], 0.0)

            def body(j, carry):
                quad = quad_of(j, bit)
                rows = [None] * 4
                for a in range(2):
                    spans = (quad[a], quad[2 + a])
                    inner = jnp.concatenate([masked(fa_ref, 2 * s, c) for c in spans], axis=0)
                    outer = jnp.concatenate([masked(fb_ref, 2 * s + 1, c) for c in spans], axis=0)
                    outer = jnp.concatenate([jnp.where(lane < span, outer, 0.0), jnp.where(lane < span, 0.0, outer)], axis=0)
                    both = jnp.dot(three(*split(outer), 1), three(*split(inner), 0), preferred_element_type=F32)
                    both = jnp.concatenate([both[: 2 * span], both[2 * span :]], axis=1)
                    rows[a], rows[2 + a] = both[:span], both[span:]
                merged = jnp.concatenate(rows, axis=0)
                for out, value in ((g_ref, merged), (t_ref, merged.T)):
                    high, low = split(value)
                    out[0, j, 0] = high
                    out[0, j, 1] = low
                return carry

            lax.fori_loop(0, g_ref.shape[1], body, 0, unroll=4)


def merge_columns_kernel(first_bit, last, ranks, fa_ref, fb_ref, fe_ref, w_ref, v_ref, g_ref, t_ref):
    span = fa_ref.shape[-2]
    row_ids = lax.broadcasted_iota(jnp.int32, (span, 2 * span), 0)

    @pl.when(pl.program_id(0) == 0)
    def _():
        for j in range(w_ref.shape[0]):
            pair = pair_of(j, last)
            factor = jnp.concatenate([jnp.where(row_ids < ranks[last, 0, c], fe_ref[0, c], 0.0) for c in pair], axis=0)
            w_ref[j] = jnp.concatenate(split(factor), axis=0)
            v_ref[j] = jnp.concatenate(split(factor.T), axis=0)

    merge_kernel(first_bit, ranks, fa_ref, fb_ref, g_ref, t_ref)


def merge_rows_kernel(first_bit, ranks, fa_ref, fb_ref, weight_ref, b_ref, g_ref, t_ref):
    @pl.when(pl.program_id(0) == 0)
    def _():
        size = weight_ref.shape[1]
        for n in range(weight_ref.shape[0]):
            b_ref[n * size : (n + 1) * size, :] = jnp.broadcast_to(weight_ref[n : n + 1, :], (size, size)).T

    merge_kernel(first_bit, ranks, fa_ref, fb_ref, g_ref, t_ref)


def level_spec(factors, index):
    return pl.BlockSpec((None, 1) + factors.shape[2:], lambda s: (0, index(s), 0, 0, 0))


def merged_shapes(factors):
    quads, side = factors.shape[2] // 4, 4 * factors.shape[3]
    shape = jax.ShapeDtypeStruct((2, quads, 2, side, side), BF16)
    return shape, pl.BlockSpec((1, quads, 2, side, side), lambda s: (s, 0, 0, 0, 0))


def merge_columns(factors, ranks):
    shape, spec = merged_shapes(factors)
    last = factors.shape[1] - 1
    pairs, width = factors.shape[2] // 2, 2 * factors.shape[3]
    single = jax.ShapeDtypeStruct((pairs, 2 * width, width), BF16)
    single_spec = pl.BlockSpec(single.shape, lambda s: (0, 0, 0))
    return pl.pallas_call(
        functools.partial(merge_columns_kernel, 0, last),
        grid=(2,),
        out_shape=(single, single, shape, shape),
        in_specs=[SMEM]
        + [level_spec(factors, f) for f in (lambda s: 2 * s, lambda s: 2 * s + 1, lambda s: last)],
        out_specs=(single_spec, single_spec, spec, spec),
        compiler_params=PARAMS,
        cost_estimate=pl.CostEstimate(flops=10**10, transcendentals=0, bytes_accessed=15 << 20),
        name="merge_columns",
    )(ranks, factors, factors, factors)


def merge_rows(factors, ranks, weights, first_bit):
    shape, spec = merged_shapes(factors)
    weights = weights.reshape(-1, 128)
    rows = weights.size
    return pl.pallas_call(
        functools.partial(merge_rows_kernel, first_bit),
        grid=(2,),
        out_shape=(jax.ShapeDtypeStruct((rows, 128), F32), shape, shape),
        in_specs=[SMEM] + [level_spec(factors, f) for f in (lambda s: 2 * s, lambda s: 2 * s + 1)] + [whole2(weights.shape)],
        out_specs=(whole2((rows, 128)), spec, spec),
        compiler_params=PARAMS,
        cost_estimate=pl.CostEstimate(flops=10**10, transcendentals=0, bytes_accessed=12 << 20),
        name="merge_rows",
    )(ranks, factors, factors, weights)


def whole2(shape):
    return pl.BlockSpec(shape, lambda s: (0, 0))


def quad_product(g_ref, x):
    return jnp.dot(three(g_ref[0], g_ref[1], 1), three(*split(x), 0), preferred_element_type=F32)


def start_merged(copies, g_ref, g_buf, stage):
    size = g_buf.shape[1] // PARTS
    return [copies.start(g_ref.at[stage, pl.ds(p * size, size)], g_buf.at[stage, pl.ds(p * size, size)]) for p in range(PARTS)]


def quad_stage(g_buf, stage, bit, load, store, ready, done=None):
    size = g_buf.shape[1] // PARTS
    for p in range(PARTS):
        ready(p)
        for j in range(p * size, (p + 1) * size):
            quad = quad_of(j, bit)
            store(quad, quad_product(g_buf.at[stage, j], load(quad)))
        if done:
            done(p)


def merged_column_kernel(back, chunk, x_ref, w_ref, g_ref, *rest):
    o_ref, x_buf, w_buf, g_buf, buf_a, buf_b, o_buf, sems = rest[-8:]
    span = w_buf.shape[-1] // 2
    rows, columns = x_buf.shape
    at = pl.ds(chunk * columns, columns)
    copies = Copies(sems)
    w_size = w_buf.shape[0] // PARTS
    start_single = lambda p: copies.start(w_ref.at[pl.ds(p * w_size, w_size)], w_buf.at[pl.ds(p * w_size, w_size)])
    run_in, run_out = part_rows(rows, 2 if back else 1), part_rows(rows, 1 if back else 2)
    get = lambda p: [copies.start(x_ref.at[r] if back else x_ref.at[r, at], x_buf.at[r]) for r in run_in[p]]
    outs = []

    def leave(p):
        for r in run_out[p]:
            outs.append(copies.start(o_buf.at[r], o_ref.at[r, at] if back else o_ref.at[r]))

    def pairs(source, target, ready, done):
        for p in range(PARTS):
            ready(p)
            for j in range(p * w_size, (p + 1) * w_size):
                pair = pair_of(j, 4)
                high, low = w_buf[j, : 2 * span], w_buf[j, 2 * span :]
                put(target, pair, span, pair_product(high, low, take(source, pair, span)))
            done(p)

    def quads(stage, bit, source, target, ready, done=None):
        quad_stage(
            g_buf, stage, bit,
            lambda quad: take(source, quad, span), lambda quad, value: put(target, quad, span, value), ready, done,
        )

    if back:
        entry = [get(p) + [start_single(p)] for p in range(PARTS)]
        g_copies = {stage: start_merged(copies, g_ref, g_buf, stage) for stage in (1, 0)}
        pairs(x_buf, buf_a, lambda p: wait_all(entry[p]), lambda p: None)
        quads(1, 2, buf_a, buf_b, lambda p: g_copies[1][p].wait())
        quads(0, 0, buf_b, o_buf, lambda p: g_copies[0][p].wait(), leave)
    else:
        size = g_buf.shape[1] // PARTS
        entry = []
        for p in range(PARTS):
            g_part = copies.start(g_ref.at[0, pl.ds(p * size, size)], g_buf.at[0, pl.ds(p * size, size)])
            entry.append(get(p) + [g_part])
        g_copies = start_merged(copies, g_ref, g_buf, 1)
        singles = [start_single(p) for p in range(PARTS)]
        quads(0, 0, x_buf, buf_a, lambda p: wait_all(entry[p]))
        quads(1, 2, buf_a, buf_b, lambda p: g_copies[p].wait())
        pairs(buf_b, o_buf, lambda p: singles[p].wait(), leave)
    wait_all(outs)


def merged_columns(x, single, merged, back, columns, chunk=0, into=None, total=None, after=()):
    rows = x.shape[0]
    extra = list(after) if into is None else [into] + list(after)
    return pl.pallas_call(
        functools.partial(merged_column_kernel, back, chunk),
        out_shape=jax.ShapeDtypeStruct((rows, total or columns), F32),
        in_specs=[HBM] * 3 + [pl.BlockSpec(memory_space=pl.ANY)] * len(extra),
        out_specs=HBM,
        scratch_shapes=[pltpu.VMEM((rows, columns), F32), pltpu.VMEM(single.shape, BF16), pltpu.VMEM(merged.shape, BF16)]
        + [pltpu.VMEM((rows, columns), F32)] * 3
        + [pltpu.SemaphoreType.DMA((32,))],
        input_output_aliases={} if into is None else {3: 0},
        compiler_params=PARAMS,
        cost_estimate=pl.CostEstimate(flops=4 * 10**9, transcendentals=0, bytes_accessed=9 << 20),
        name="column_back" if back else "column_tree_merged",
    )(x, single, merged, *extra)


def row_kernel(first_bit, span, place, x_ref, g_ref, keep_ref, send_ref, x_buf, g_buf, buf, keep_buf, send_buf, sems):
    swap = place[1] == 1
    rows = x_buf.shape[0]
    copies = Copies(sems)
    size = g_buf.shape[1] // PARTS
    entry, outs = [], []
    for p in range(PARTS):
        r = part_rows(rows, 1)[p][0]
        g_part = copies.start(g_ref.at[0, pl.ds(p * size, size)], g_buf.at[0, pl.ds(p * size, size)])
        entry.append([g_part, copies.start(x_ref.at[r], x_buf.at[r])])
    g_copies = start_merged(copies, g_ref, g_buf, 1)

    def store(quad, value):
        half = 2 * span
        low, high = value[:half], value[half:]
        put(keep_buf, quad[:2], span, jnp.where(swap, high, low))
        put(send_buf, quad[:2], span, jnp.where(swap, low, high))

    def leave(p):
        for r in part_rows(rows // 2, 2)[p]:
            outs.append(copies.start(send_buf.at[r], send_ref.at[r]))
            outs.append(copies.start(keep_buf.at[r], keep_ref.at[r]))

    load = lambda ref: lambda quad: take(ref, quad, span)
    quad_stage(
        g_buf, 0, first_bit, load(x_buf), lambda quad, value: put(buf, quad, span, value), lambda p: wait_all(entry[p])
    )
    quad_stage(g_buf, 1, first_bit + 2, load(buf), store, lambda p: g_copies[p].wait(), leave)
    wait_all(outs)


def row_tree(x, merged, place, first_bit, span):
    rows, columns = x.shape
    half = jax.ShapeDtypeStruct((rows // 2, columns), F32)
    return pl.pallas_call(
        functools.partial(row_kernel, first_bit, span),
        out_shape=(half, half),
        in_specs=[SMEM0, HBM, HBM],
        out_specs=(HBM, HBM),
        scratch_shapes=[pltpu.VMEM((rows, columns), F32), pltpu.VMEM(merged.shape, BF16), pltpu.VMEM((rows, columns), F32)]
        + [pltpu.VMEM(half.shape, F32)] * 2
        + [pltpu.SemaphoreType.DMA((32,))],
        compiler_params=PARAMS,
        cost_estimate=pl.CostEstimate(flops=3 * 10**9, transcendentals=0, bytes_accessed=8 << 20),
        name="row_tree",
    )(place, x, merged)


def add_halves_kernel(ring, place, keep_ref, got_ref, *refs):
    outs, (k_buf, g_buf, in_sems, out_sems) = refs[:ring], refs[ring:]
    size = outs[0].shape[0]
    copies = []
    for d in range(ring):
        rows = pl.ds(pl.multiple_of(lax.rem(place[0] + d, ring) * size, size), size)
        copies.append(pltpu.make_async_copy(keep_ref.at[rows], k_buf.at[d], in_sems.at[0, d]))
        copies.append(pltpu.make_async_copy(got_ref.at[rows], g_buf.at[d], in_sems.at[1, d]))
    for copy in copies:
        copy.start()
    sends = []
    for d, out in enumerate(outs):
        copies[2 * d].wait()
        copies[2 * d + 1].wait()
        g_buf[d] = g_buf[d] + k_buf[d]
        sends.append(pltpu.make_async_copy(g_buf.at[d], out, out_sems.at[d]))
        sends[-1].start()
    for send in sends:
        send.wait()


def add_halves(keep, got, place, ring):
    rows, columns = keep.shape
    size = rows // ring
    piece = jax.ShapeDtypeStruct((size, columns), F32)
    return pl.pallas_call(
        functools.partial(add_halves_kernel, ring),
        out_shape=(piece,) * ring,
        in_specs=[SMEM0, HBM, HBM],
        out_specs=(HBM,) * ring,
        scratch_shapes=[pltpu.VMEM((ring, size, columns), F32)] * 2
        + [pltpu.SemaphoreType.DMA((2, ring)), pltpu.SemaphoreType.DMA((ring,))],
        compiler_params=PARAMS,
        cost_estimate=pl.CostEstimate(flops=keep.size, transcendentals=0, bytes_accessed=12 * keep.size),
        name="add_halves",
    )(place, keep, got)


def add_pieces_kernel(count, *refs):
    pieces, out = refs[:count], refs[count]
    buf, in_sems, out_sems = refs[count + 1 :]
    parts = buf.shape[1]
    size = out.shape[0] // parts
    copies = []
    for p in range(parts):
        for n, piece in enumerate(pieces):
            copies.append(pltpu.make_async_copy(piece.at[pl.ds(p * size, size)], buf.at[n, p], in_sems.at[n, p]))
            copies[-1].start()
    sends = []
    for p in range(parts):
        for n in range(count):
            copies[p * count + n].wait()
        total = buf[0, p]
        for n in range(1, count):
            total = total + buf[n, p]
        buf[0, p] = total
        sends.append(pltpu.make_async_copy(buf.at[0, p], out.at[pl.ds(p * size, size)], out_sems.at[p]))
        sends[-1].start()
    for send in sends:
        send.wait()


def add_pieces(pieces):
    rows, columns = pieces[0].shape
    count, parts = len(pieces), 2
    return pl.pallas_call(
        functools.partial(add_pieces_kernel, count),
        out_shape=jax.ShapeDtypeStruct((rows, columns), F32),
        in_specs=[HBM] * count,
        out_specs=HBM,
        scratch_shapes=[pltpu.VMEM((count, parts, rows // parts, columns), F32)]
        + [pltpu.SemaphoreType.DMA((count, parts)), pltpu.SemaphoreType.DMA((parts,))],
        compiler_params=PARAMS,
        cost_estimate=pl.CostEstimate(flops=4 * pieces[0].size, transcendentals=0, bytes_accessed=20 * pieces[0].size),
        name="add_pieces",
    )(*pieces)


def weigh_kernel(first_bit, span, ring, chunk, place, *refs):
    pieces = refs[: 2 * ring]
    w_ref, g_ref = refs[2 * ring : 2 * ring + 2]
    b_ref, o_ref, x_buf, w_buf, g_buf, buf, o_buf, sems = refs[-8:]
    size, columns = pieces[0].shape
    rows = x_buf.shape[0]
    copies = Copies(sems)
    entry, outs = [], []
    for n, piece in enumerate(pieces):
        side, d = divmod(n, ring)
        half = place[1] if side == 0 else 1 - place[1]
        begin = half * (ring * size) + lax.rem(place[0] + ring - d, ring) * size
        entry.append(copies.start(piece, x_buf.at[pl.ds(pl.multiple_of(begin, size), size)]))
    entry.append(copies.start(w_ref, w_buf))
    g_copies = {stage: start_merged(copies, g_ref, g_buf, stage) for stage in (1, 0)}
    wait_all(entry)
    block_out = copies.start(x_buf, b_ref.at[:, pl.ds(chunk * columns, columns)])

    def weighted(quad):
        value, weight = take(x_buf, quad, span), take(w_buf, quad, span)
        return value * jnp.concatenate([weight] * (columns // weight.shape[1]), axis=1)

    def leave(p):
        r = part_rows(rows, 1)[p][0]
        outs.append(copies.start(o_buf.at[r], o_ref.at[r]))

    quad_stage(
        g_buf, 1, first_bit + 2, weighted, lambda quad, value: put(buf, quad, span, value), lambda p: g_copies[1][p].wait()
    )
    quad_stage(
        g_buf, 0, first_bit, lambda quad: take(buf, quad, span),
        lambda quad, value: put(o_buf, quad, span, value), lambda p: g_copies[0][p].wait(), leave,
    )
    wait_all(outs + [block_out])


def weigh_back(pieces, weights, merged, place, first_bit, span, into, chunk, total):
    ring = len(pieces) // 2
    size, columns = pieces[0].shape
    rows = 2 * ring * size
    extra = [] if into is None else [into]
    return pl.pallas_call(
        functools.partial(weigh_kernel, first_bit, span, ring, chunk),
        out_shape=(jax.ShapeDtypeStruct((rows, total), F32), jax.ShapeDtypeStruct((rows, columns), F32)),
        in_specs=[SMEM0] + [HBM] * (len(pieces) + 2 + len(extra)),
        out_specs=(HBM, HBM),
        scratch_shapes=[pltpu.VMEM((rows, columns), F32), pltpu.VMEM(weights.shape, F32), pltpu.VMEM(merged.shape, BF16)]
        + [pltpu.VMEM((rows, columns), F32)] * 2
        + [pltpu.SemaphoreType.DMA((32,))],
        input_output_aliases={3 + len(pieces): 0} if extra else {},
        compiler_params=PARAMS,
        cost_estimate=pl.CostEstimate(flops=3 * 10**9, transcendentals=0, bytes_accessed=12 << 20),
        name="weigh_back",
    )(place, *pieces, weights, merged, *extra)


def exchange(x):
    nodes = lax.axis_size("node")
    rows, columns = x.shape
    out = lax.all_to_all(x.reshape(nodes, rows // nodes, columns), "node", split_axis=0, concat_axis=0, tiled=True)
    return out.reshape(rows, columns)


def shards(vectors, col_factors, row_factors, col_ranks, row_ranks, row_weights):
    rows, total = vectors.shape[1:]
    columns = total // CHUNKS
    low_bits = col_factors.shape[1] - row_factors.shape[1]
    ring = lax.axis_size("block") // 2
    sibling = [(b, b ^ 1) for b in range(2 * ring)]
    shift = [[(b, (b + 2 * d) % (2 * ring)) for b in range(2 * ring)] for d in range(ring)]
    index = lax.axis_index("block")
    place = jnp.stack([index // 2, index % 2]).astype(jnp.int32)
    span = col_factors.shape[3]
    flat = vectors.reshape(rows, total)
    col_ranks = jnp.transpose(col_ranks, (1, 0, 2))
    row_ranks = jnp.transpose(row_ranks, (1, 0, 2))
    chunks = range(CHUNKS)
    t = column_tree(flat, col_factors, col_ranks, columns, 0)
    sent = [exchange(t)]
    single, single_back, col_merged, col_back = merge_columns(col_factors, col_ranks)
    weights, row_merged, row_back = merge_rows(row_factors, row_ranks, row_weights, low_bits)
    for n in chunks[1:]:
        t = merged_columns(flat, single, col_merged, False, columns, n, after=[weights])
        sent.append(exchange(t))
    halves = []
    for n in chunks:
        halves.append(row_tree(sent[n], row_merged, place, low_bits, span))

    def start(n):
        got = lax.ppermute(halves[n][1], "block", sibling)
        return add_halves(halves[n][0], got, place, ring)

    block_row = result = None
    back = []
    pieces = start(0)
    for n in chunks:
        later = n + 1 < CHUNKS
        got = [pieces[0]]
        for d in range(1, ring):
            got.append(lax.ppermute(pieces[d], "block", shift[d]))
        total_piece = add_pieces(got)
        mine = [total_piece]
        for d in range(1, ring):
            mine.append(lax.ppermute(total_piece, "block", shift[d]))
        if later:
            pieces = start(n + 1)
            mine[1:], pieces = lax.optimization_barrier((mine[1:], pieces))
        theirs = [lax.ppermute(piece, "block", sibling) for piece in mine]
        block_row, t = weigh_back(mine + theirs, weights, row_back, place, low_bits, span, block_row, n, total)
        back.append(exchange(t))
    for n in chunks:
        result = merged_columns(back[n], single_back, col_back, True, columns, n, result, total)
    return block_row, result.reshape(1, rows, total)


def solution(mesh):
    in_specs = (
        P("block", "node", None),
        P("block", None, "node", None, None),
        P("block", None, "node", None, None),
        P("block", None, "node"),
        P("block", None, "node"),
        P("node"),
    )
    out_specs = (P("node", None), P("block", "node", None))
    return jax.shard_map(shards, mesh=mesh, in_specs=in_specs, out_specs=out_specs, check_vma=False)
```

```python
import functools
import jax
import jax.numpy as jnp
from jax import lax
from jax.experimental import pallas as pl
from jax.experimental.pallas import tpu as pltpu
from jax.sharding import PartitionSpec as P


CHUNKS = 2
F32 = jnp.float32
BF16 = jnp.bfloat16
PARAMS = pltpu.CompilerParams(vmem_limit_bytes=67043328)
ROW_PARAMS = pltpu.CompilerParams(vmem_limit_bytes=96 << 19)
WEIGH_PARAMS = pltpu.CompilerParams(vmem_limit_bytes=112 << 19)
SUM_PARAMS = pltpu.CompilerParams(vmem_limit_bytes=48 << 20)


def split(value):
    high = value.astype(jnp.bfloat16)
    low = (value - high.astype(F32)).astype(jnp.bfloat16)
    return high, low


def pair_of(j, bit):
    first = ((j >> bit) << (bit + 1)) + (j & ((1 << bit) - 1))
    return first, first + (1 << bit)


PARTS = 4


def rows_of(c, span):
    return slice(c * span, (c + 1) * span)


def take(ref, spans, span):
    return jnp.concatenate([ref[rows_of(c, span), :] for c in spans], axis=0)


def put(ref, spans, span, value):
    for n, c in enumerate(spans):
        ref[rows_of(c, span), :] = value[n * span : (n + 1) * span]


class Copies:
    def __init__(self, sems):
        self.sems, self.used = sems, 0

    def start(self, source, target):
        copy = pltpu.make_async_copy(source, target, self.sems.at[self.used])
        self.used += 1
        copy.start()
        return copy


def wait_all(copies):
    for copy in copies:
        copy.wait()


def part_rows(rows, halves):
    size = rows // PARTS // halves
    return [[pl.ds(h * (rows // halves) + p * size, size) for h in range(halves)] for p in range(PARTS)]


def pair_product(f_high, f_low, x):
    lhs = jnp.concatenate([f_high, f_low], axis=0)
    lhs = jnp.concatenate([lhs, lhs], axis=1)
    out = jnp.dot(lhs, jnp.concatenate(split(x), axis=0), preferred_element_type=F32)
    half = out.shape[0] // 2
    return out[:half] + out[half:]


def column_kernel(chunk, ranks, x_ref, f_ref, o_ref, x_buf, f_buf, buf_a, buf_b, o_buf, sems):
    levels, count, span = f_buf.shape[:3]
    rows, columns = x_buf.shape
    copies = Copies(sems)
    at = pl.ds(chunk * columns, columns)
    first = []
    size = count // PARTS
    for p in range(PARTS):
        first.append(
            [
                copies.start(f_ref.at[0, 0, pl.ds(p * size, size)], f_buf.at[0, pl.ds(p * size, size)]),
                copies.start(x_ref.at[pl.ds(p * size * span, size * span), at], x_buf.at[pl.ds(p * size * span, size * span)]),
            ]
        )
    later = [copies.start(f_ref.at[0, level], f_buf.at[level]) for level in range(1, levels)]
    bufs = [x_buf] + [(buf_a, buf_b)[level % 2] for level in range(levels - 1)] + [o_buf]
    row_ids = lax.broadcasted_iota(jnp.int32, (span, 2 * span), 0)
    outs = []
    for level in range(levels):
        if level:
            later[level - 1].wait()
        for p in range(PARTS):
            if level == 0:
                wait_all(first[p])
            for j in range(p * size // 2, (p + 1) * size // 2):
                pair = pair_of(j, level)
                factor = jnp.concatenate(
                    [jnp.where(row_ids < ranks[level, 0, c], f_buf[level, c], 0.0) for c in pair], axis=0
                )
                put(bufs[level + 1], pair, span, pair_product(*split(factor), take(bufs[level], pair, span)))
            if level == levels - 1:
                outs += [copies.start(o_buf.at[at], o_ref.at[at]) for at in part_rows(rows, 2)[p]]
    wait_all(outs)


def column_tree(x, factors, ranks, columns, chunk):
    rows = x.shape[0]
    return pl.pallas_call(
        functools.partial(column_kernel, chunk),
        out_shape=jax.ShapeDtypeStruct((rows, columns), F32),
        in_specs=[SMEM0, HBM, HBM],
        out_specs=HBM,
        scratch_shapes=[pltpu.VMEM((rows, columns), F32), pltpu.VMEM(factors.shape[1:], F32)]
        + [pltpu.VMEM((rows, columns), F32)] * 3
        + [pltpu.SemaphoreType.DMA((32,))],
        compiler_params=PARAMS,
        cost_estimate=pl.CostEstimate(flops=5 * 10**9, transcendentals=0, bytes_accessed=9 << 20),
        name="column_tree",
    )(ranks, x, factors)


SMEM0 = pl.BlockSpec(memory_space=pltpu.SMEM)
HBM = pl.BlockSpec(memory_space=pltpu.HBM)
ANYWHERE = pl.BlockSpec(memory_space=pl.ANY)
SMEM = SMEM0


def quad_of(j, bit):
    base = ((j >> bit) << (bit + 2)) + (j & ((1 << bit) - 1))
    return [base + (n << bit) for n in range(4)]


def three(high, low, axis):
    return jnp.concatenate([high, high, low] if axis == 1 else [high, low, high], axis=axis)


def merge_kernel(first_bit, ranks, fa_ref, fb_ref, *refs):
    g_ref, t_ref = refs[-2:]
    span = fa_ref.shape[-2]
    lane = lax.broadcasted_iota(jnp.int32, (2 * span, 2 * span), 1)
    row_ids = lax.broadcasted_iota(jnp.int32, (span, 2 * span), 0)
    for s in range(2):

        @pl.when(pl.program_id(0) == s)
        def _(s=s):
            bit = first_bit + 2 * s
            masked = lambda ref, level, c: jnp.where(row_ids < ranks[level, 0, c], ref[0, c], 0.0)

            def body(j, carry):
                quad = quad_of(j, bit)
                rows = [None] * 4
                for a in range(2):
                    spans = (quad[a], quad[2 + a])
                    inner = jnp.concatenate([masked(fa_ref, 2 * s, c) for c in spans], axis=0)
                    outer = jnp.concatenate([masked(fb_ref, 2 * s + 1, c) for c in spans], axis=0)
                    outer = jnp.concatenate([jnp.where(lane < span, outer, 0.0), jnp.where(lane < span, 0.0, outer)], axis=0)
                    both = jnp.dot(three(*split(outer), 1), three(*split(inner), 0), preferred_element_type=F32)
                    both = jnp.concatenate([both[: 2 * span], both[2 * span :]], axis=1)
                    rows[a], rows[2 + a] = both[:span], both[span:]
                merged = jnp.concatenate(rows, axis=0)
                for out, value in ((g_ref, merged), (t_ref, merged.T)):
                    high, low = split(value)
                    out[0, j, 0] = high
                    out[0, j, 1] = low
                return carry

            lax.fori_loop(0, g_ref.shape[1], body, 0, unroll=4)


def merge_columns_kernel(first_bit, last, ranks, fa_ref, fb_ref, fe_ref, w_ref, v_ref, g_ref, t_ref):
    span = fa_ref.shape[-2]
    row_ids = lax.broadcasted_iota(jnp.int32, (span, 2 * span), 0)

    @pl.when(pl.program_id(0) == 0)
    def _():
        for j in range(w_ref.shape[0]):
            pair = pair_of(j, last)
            factor = jnp.concatenate([jnp.where(row_ids < ranks[last, 0, c], fe_ref[0, c], 0.0) for c in pair], axis=0)
            w_ref[j] = jnp.concatenate(split(factor), axis=0)
            v_ref[j] = jnp.concatenate(split(factor.T), axis=0)

    merge_kernel(first_bit, ranks, fa_ref, fb_ref, g_ref, t_ref)


def merge_rows_kernel(first_bit, ranks, fa_ref, fb_ref, weight_ref, b_ref, g_ref, t_ref):
    @pl.when(pl.program_id(0) == 0)
    def _():
        size = weight_ref.shape[1]
        for n in range(weight_ref.shape[0]):
            b_ref[n * size : (n + 1) * size, :] = jnp.broadcast_to(weight_ref[n : n + 1, :], (size, size)).T

    merge_kernel(first_bit, ranks, fa_ref, fb_ref, g_ref, t_ref)


def level_spec(factors, index):
    return pl.BlockSpec((None, 1) + factors.shape[2:], lambda s: (0, index(s), 0, 0, 0))


def merged_shapes(factors):
    quads, side = factors.shape[2] // 4, 4 * factors.shape[3]
    shape = jax.ShapeDtypeStruct((2, quads, 2, side, side), BF16)
    return shape, pl.BlockSpec((1, quads, 2, side, side), lambda s: (s, 0, 0, 0, 0))


def merge_columns(factors, ranks):
    shape, spec = merged_shapes(factors)
    last = factors.shape[1] - 1
    pairs, width = factors.shape[2] // 2, 2 * factors.shape[3]
    single = jax.ShapeDtypeStruct((pairs, 2 * width, width), BF16)
    single_spec = pl.BlockSpec(single.shape, lambda s: (0, 0, 0))
    return pl.pallas_call(
        functools.partial(merge_columns_kernel, 0, last),
        grid=(2,),
        out_shape=(single, single, shape, shape),
        in_specs=[SMEM]
        + [level_spec(factors, f) for f in (lambda s: 2 * s, lambda s: 2 * s + 1, lambda s: last)],
        out_specs=(single_spec, single_spec, spec, spec),
        compiler_params=PARAMS,
        cost_estimate=pl.CostEstimate(flops=10**10, transcendentals=0, bytes_accessed=15 << 20),
        name="merge_columns",
    )(ranks, factors, factors, factors)


def merge_rows(factors, ranks, weights, first_bit):
    shape, spec = merged_shapes(factors)
    weights = weights.reshape(-1, 128)
    rows = weights.size
    return pl.pallas_call(
        functools.partial(merge_rows_kernel, first_bit),
        grid=(2,),
        out_shape=(jax.ShapeDtypeStruct((rows, 128), F32), shape, shape),
        in_specs=[SMEM] + [level_spec(factors, f) for f in (lambda s: 2 * s, lambda s: 2 * s + 1)] + [whole2(weights.shape)],
        out_specs=(whole2((rows, 128)), spec, spec),
        compiler_params=PARAMS,
        cost_estimate=pl.CostEstimate(flops=10**10, transcendentals=0, bytes_accessed=12 << 20),
        name="merge_rows",
    )(ranks, factors, factors, weights)


def whole2(shape):
    return pl.BlockSpec(shape, lambda s: (0, 0))


def quad_product(g_ref, x):
    return jnp.dot(three(g_ref[0], g_ref[1], 1), three(*split(x), 0), preferred_element_type=F32)


def start_merged(copies, g_ref, g_buf, stage):
    size = g_buf.shape[1] // PARTS
    return [copies.start(g_ref.at[stage, pl.ds(p * size, size)], g_buf.at[stage, pl.ds(p * size, size)]) for p in range(PARTS)]


def quad_stage(g_buf, stage, bit, load, store, ready, done=None):
    size = g_buf.shape[1] // PARTS
    for p in range(PARTS):
        ready(p)
        for j in range(p * size, (p + 1) * size):
            quad = quad_of(j, bit)
            store(quad, quad_product(g_buf.at[stage, j], load(quad)))
        if done:
            done(p)


def merged_column_kernel(back, chunk, x_ref, w_ref, g_ref, *rest):
    o_ref, x_buf, w_buf, g_buf, buf_a, buf_b, o_buf, sems = rest[-8:]
    span = w_buf.shape[-1] // 2
    rows, columns = x_buf.shape
    at = pl.ds(chunk * columns, columns)
    copies = Copies(sems)
    w_size = w_buf.shape[0] // PARTS
    start_single = lambda p: copies.start(w_ref.at[pl.ds(p * w_size, w_size)], w_buf.at[pl.ds(p * w_size, w_size)])
    run_in, run_out = part_rows(rows, 2 if back else 1), part_rows(rows, 1 if back else 2)
    get = lambda p: [copies.start(x_ref.at[r] if back else x_ref.at[r, at], x_buf.at[r]) for r in run_in[p]]
    outs = []

    def leave(p):
        for r in run_out[p]:
            outs.append(copies.start(o_buf.at[r], o_ref.at[r, at] if back else o_ref.at[r]))

    def pairs(source, target, ready, done):
        for p in range(PARTS):
            ready(p)
            for j in range(p * w_size, (p + 1) * w_size):
                pair = pair_of(j, 4)
                high, low = w_buf[j, : 2 * span], w_buf[j, 2 * span :]
                put(target, pair, span, pair_product(high, low, take(source, pair, span)))
            done(p)

    def quads(stage, bit, source, target, ready, done=None):
        quad_stage(
            g_buf, stage, bit,
            lambda quad: take(source, quad, span), lambda quad, value: put(target, quad, span, value), ready, done,
        )

    if back:
        entry = [get(p) + [start_single(p)] for p in range(PARTS)]
        g_copies = {stage: start_merged(copies, g_ref, g_buf, stage) for stage in (1, 0)}
        pairs(x_buf, buf_a, lambda p: wait_all(entry[p]), lambda p: None)
        quads(1, 2, buf_a, buf_b, lambda p: g_copies[1][p].wait())
        quads(0, 0, buf_b, o_buf, lambda p: g_copies[0][p].wait(), leave)
    else:
        size = g_buf.shape[1] // PARTS
        entry = []
        for p in range(PARTS):
            g_part = copies.start(g_ref.at[0, pl.ds(p * size, size)], g_buf.at[0, pl.ds(p * size, size)])
            entry.append(get(p) + [g_part])
        g_copies = start_merged(copies, g_ref, g_buf, 1)
        singles = [start_single(p) for p in range(PARTS)]
        quads(0, 0, x_buf, buf_a, lambda p: wait_all(entry[p]))
        quads(1, 2, buf_a, buf_b, lambda p: g_copies[p].wait())
        pairs(buf_b, o_buf, lambda p: singles[p].wait(), leave)
    wait_all(outs)


def merged_columns(x, single, merged, back, columns, chunk=0, into=None, total=None, after=()):
    rows = x.shape[0]
    extra = list(after) if into is None else [into] + list(after)
    return pl.pallas_call(
        functools.partial(merged_column_kernel, back, chunk),
        out_shape=jax.ShapeDtypeStruct((rows, total or columns), F32),
        in_specs=[HBM] * 3 + [pl.BlockSpec(memory_space=pl.ANY)] * len(extra),
        out_specs=HBM,
        scratch_shapes=[pltpu.VMEM((rows, columns), F32), pltpu.VMEM(single.shape, BF16), pltpu.VMEM(merged.shape, BF16)]
        + [pltpu.VMEM((rows, columns), F32)] * 3
        + [pltpu.SemaphoreType.DMA((32,))],
        input_output_aliases={} if into is None else {3: 0},
        compiler_params=PARAMS,
        cost_estimate=pl.CostEstimate(flops=4 * 10**9, transcendentals=0, bytes_accessed=9 << 20),
        name="column_back" if back else "column_tree_merged",
    )(x, single, merged, *extra)


def row_kernel(first_bit, span, place, x_ref, g_ref, keep_ref, send_ref, x_buf, g_buf, buf, keep_buf, send_buf, sems):
    swap = place[1] == 1
    rows = x_buf.shape[0]
    copies = Copies(sems)
    size = g_buf.shape[1] // PARTS
    entry, outs = [], []
    for p in range(PARTS):
        r = part_rows(rows, 1)[p][0]
        g_part = copies.start(g_ref.at[0, pl.ds(p * size, size)], g_buf.at[0, pl.ds(p * size, size)])
        entry.append([g_part, copies.start(x_ref.at[r], x_buf.at[r])])
    g_copies = start_merged(copies, g_ref, g_buf, 1)

    def store(quad, value):
        half = 2 * span
        low, high = value[:half], value[half:]
        put(keep_buf, quad[:2], span, jnp.where(swap, high, low))
        put(send_buf, quad[:2], span, jnp.where(swap, low, high))

    def leave(p):
        for r in part_rows(rows // 2, 2)[p]:
            outs.append(copies.start(send_buf.at[r], send_ref.at[r]))
            outs.append(copies.start(keep_buf.at[r], keep_ref.at[r]))

    load = lambda ref: lambda quad: take(ref, quad, span)
    quad_stage(
        g_buf, 0, first_bit, load(x_buf), lambda quad, value: put(buf, quad, span, value), lambda p: wait_all(entry[p])
    )
    quad_stage(g_buf, 1, first_bit + 2, load(buf), store, lambda p: g_copies[p].wait(), leave)
    wait_all(outs)


def row_tree(x, merged, place, first_bit, span):
    rows, columns = x.shape
    half = jax.ShapeDtypeStruct((rows // 2, columns), F32)
    return pl.pallas_call(
        functools.partial(row_kernel, first_bit, span),
        out_shape=(half, half),
        in_specs=[SMEM0, HBM, HBM],
        out_specs=(ANYWHERE, ANYWHERE),
        scratch_shapes=[pltpu.VMEM((rows, columns), F32), pltpu.VMEM(merged.shape, BF16), pltpu.VMEM((rows, columns), F32)]
        + [pltpu.VMEM(half.shape, F32)] * 2
        + [pltpu.SemaphoreType.DMA((32,))],
        compiler_params=ROW_PARAMS,
        cost_estimate=pl.CostEstimate(flops=3 * 10**9, transcendentals=0, bytes_accessed=8 << 20),
        name="row_tree",
    )(place, x, merged)


def add_halves_kernel(ring, place, keep_ref, got_ref, *refs):
    outs, (k_buf, g_buf, in_sems, out_sems) = refs[:ring], refs[ring:]
    size = outs[0].shape[0]
    copies = []
    for d in range(ring):
        rows = pl.ds(pl.multiple_of(lax.rem(place[0] + d, ring) * size, size), size)
        copies.append(pltpu.make_async_copy(keep_ref.at[rows], k_buf.at[d], in_sems.at[0, d]))
        copies.append(pltpu.make_async_copy(got_ref.at[rows], g_buf.at[d], in_sems.at[1, d]))
    for copy in copies:
        copy.start()
    sends = []
    for d, out in enumerate(outs):
        copies[2 * d].wait()
        copies[2 * d + 1].wait()
        g_buf[d] = g_buf[d] + k_buf[d]
        sends.append(pltpu.make_async_copy(g_buf.at[d], out, out_sems.at[d]))
        sends[-1].start()
    for send in sends:
        send.wait()


def add_halves(keep, got, place, ring):
    rows, columns = keep.shape
    size = rows // ring
    piece = jax.ShapeDtypeStruct((size, columns), F32)
    return pl.pallas_call(
        functools.partial(add_halves_kernel, ring),
        out_shape=(piece,) * ring,
        in_specs=[SMEM0, ANYWHERE, ANYWHERE],
        out_specs=(ANYWHERE,) * ring,
        scratch_shapes=[pltpu.VMEM((ring, size, columns), F32)] * 2
        + [pltpu.SemaphoreType.DMA((2, ring)), pltpu.SemaphoreType.DMA((ring,))],
        compiler_params=SUM_PARAMS,
        cost_estimate=pl.CostEstimate(flops=keep.size, transcendentals=0, bytes_accessed=12 * keep.size),
        name="add_halves",
    )(place, keep, got)


def add_pieces_kernel(count, *refs):
    pieces, out = refs[:count], refs[count]
    buf, in_sems, out_sems = refs[count + 1 :]
    parts = buf.shape[1]
    size = out.shape[0] // parts
    copies = []
    for p in range(parts):
        for n, piece in enumerate(pieces):
            copies.append(pltpu.make_async_copy(piece.at[pl.ds(p * size, size)], buf.at[n, p], in_sems.at[n, p]))
            copies[-1].start()
    sends = []
    for p in range(parts):
        for n in range(count):
            copies[p * count + n].wait()
        total = buf[0, p]
        for n in range(1, count):
            total = total + buf[n, p]
        buf[0, p] = total
        sends.append(pltpu.make_async_copy(buf.at[0, p], out.at[pl.ds(p * size, size)], out_sems.at[p]))
        sends[-1].start()
    for send in sends:
        send.wait()


def add_pieces(pieces):
    rows, columns = pieces[0].shape
    count, parts = len(pieces), 2
    return pl.pallas_call(
        functools.partial(add_pieces_kernel, count),
        out_shape=jax.ShapeDtypeStruct((rows, columns), F32),
        in_specs=[ANYWHERE] * count,
        out_specs=ANYWHERE,
        scratch_shapes=[pltpu.VMEM((count, parts, rows // parts, columns), F32)]
        + [pltpu.SemaphoreType.DMA((count, parts)), pltpu.SemaphoreType.DMA((parts,))],
        compiler_params=SUM_PARAMS,
        cost_estimate=pl.CostEstimate(flops=4 * pieces[0].size, transcendentals=0, bytes_accessed=20 * pieces[0].size),
        name="add_pieces",
    )(*pieces)


def weigh_kernel(first_bit, span, ring, chunk, place, *refs):
    pieces = refs[: 2 * ring]
    w_ref, g_ref = refs[2 * ring : 2 * ring + 2]
    b_ref, o_ref, x_buf, w_buf, g_buf, buf, o_buf, sems = refs[-8:]
    size, columns = pieces[0].shape
    rows = x_buf.shape[0]
    copies = Copies(sems)
    entry, outs = [], []
    for n, piece in enumerate(pieces):
        side, d = divmod(n, ring)
        half = place[1] if side == 0 else 1 - place[1]
        begin = half * (ring * size) + lax.rem(place[0] + ring - d, ring) * size
        entry.append(copies.start(piece, x_buf.at[pl.ds(pl.multiple_of(begin, size), size)]))
    entry.append(copies.start(w_ref, w_buf))
    g_copies = {stage: start_merged(copies, g_ref, g_buf, stage) for stage in (1, 0)}
    wait_all(entry)
    block_out = copies.start(x_buf, b_ref.at[:, pl.ds(chunk * columns, columns)])

    def weighted(quad):
        value, weight = take(x_buf, quad, span), take(w_buf, quad, span)
        return value * jnp.concatenate([weight] * (columns // weight.shape[1]), axis=1)

    def leave(p):
        r = part_rows(rows, 1)[p][0]
        outs.append(copies.start(o_buf.at[r], o_ref.at[r]))

    quad_stage(
        g_buf, 1, first_bit + 2, weighted, lambda quad, value: put(buf, quad, span, value), lambda p: g_copies[1][p].wait()
    )
    quad_stage(
        g_buf, 0, first_bit, lambda quad: take(buf, quad, span),
        lambda quad, value: put(o_buf, quad, span, value), lambda p: g_copies[0][p].wait(), leave,
    )
    wait_all(outs + [block_out])


def weigh_back(pieces, weights, merged, place, first_bit, span, into, chunk, total):
    ring = len(pieces) // 2
    size, columns = pieces[0].shape
    rows = 2 * ring * size
    extra = [] if into is None else [into]
    return pl.pallas_call(
        functools.partial(weigh_kernel, first_bit, span, ring, chunk),
        out_shape=(jax.ShapeDtypeStruct((rows, total), F32), jax.ShapeDtypeStruct((rows, columns), F32)),
        in_specs=[SMEM0] + [ANYWHERE] * len(pieces) + [HBM] * (2 + len(extra)),
        out_specs=(HBM, HBM),
        scratch_shapes=[pltpu.VMEM((rows, columns), F32), pltpu.VMEM(weights.shape, F32), pltpu.VMEM(merged.shape, BF16)]
        + [pltpu.VMEM((rows, columns), F32)] * 2
        + [pltpu.SemaphoreType.DMA((32,))],
        input_output_aliases={3 + len(pieces): 0} if extra else {},
        compiler_params=WEIGH_PARAMS,
        cost_estimate=pl.CostEstimate(flops=3 * 10**9, transcendentals=0, bytes_accessed=12 << 20),
        name="weigh_back",
    )(place, *pieces, weights, merged, *extra)


def exchange(x):
    nodes = lax.axis_size("node")
    rows, columns = x.shape
    out = lax.all_to_all(x.reshape(nodes, rows // nodes, columns), "node", split_axis=0, concat_axis=0, tiled=True)
    return out.reshape(rows, columns)


def shards(vectors, col_factors, row_factors, col_ranks, row_ranks, row_weights):
    rows, total = vectors.shape[1:]
    columns = total // CHUNKS
    low_bits = col_factors.shape[1] - row_factors.shape[1]
    ring = lax.axis_size("block") // 2
    sibling = [(b, b ^ 1) for b in range(2 * ring)]
    shift = [[(b, (b + 2 * d) % (2 * ring)) for b in range(2 * ring)] for d in range(ring)]
    index = lax.axis_index("block")
    place = jnp.stack([index // 2, index % 2]).astype(jnp.int32)
    span = col_factors.shape[3]
    flat = vectors.reshape(rows, total)
    col_ranks = jnp.transpose(col_ranks, (1, 0, 2))
    row_ranks = jnp.transpose(row_ranks, (1, 0, 2))
    chunks = range(CHUNKS)
    t = column_tree(flat, col_factors, col_ranks, columns, 0)
    sent = [exchange(t)]
    single, single_back, col_merged, col_back = merge_columns(col_factors, col_ranks)
    weights, row_merged, row_back = merge_rows(row_factors, row_ranks, row_weights, low_bits)
    for n in chunks[1:]:
        t = merged_columns(flat, single, col_merged, False, columns, n, after=[weights])
        sent.append(exchange(t))
    halves = []
    for n in chunks:
        halves.append(row_tree(sent[n], row_merged, place, low_bits, span))

    def start(n):
        got = lax.ppermute(halves[n][1], "block", sibling)
        return add_halves(halves[n][0], got, place, ring)

    block_row = result = None
    back = []
    pieces = start(0)
    for n in chunks:
        later = n + 1 < CHUNKS
        got = [pieces[0]]
        for d in range(1, ring):
            got.append(lax.ppermute(pieces[d], "block", shift[d]))
        total_piece = add_pieces(got)
        mine = [total_piece]
        for d in range(1, ring):
            mine.append(lax.ppermute(total_piece, "block", shift[d]))
        if later:
            pieces = start(n + 1)
            mine[1:], pieces = lax.optimization_barrier((mine[1:], pieces))
        theirs = [lax.ppermute(piece, "block", sibling) for piece in mine]
        block_row, t = weigh_back(mine + theirs, weights, row_back, place, low_bits, span, block_row, n, total)
        back.append(exchange(t))
    for n in chunks:
        result = merged_columns(back[n], single_back, col_back, True, columns, n, result, total)
    return block_row, result.reshape(1, rows, total)


def solution(mesh):
    in_specs = (
        P("block", "node", None),
        P("block", None, "node", None, None),
        P("block", None, "node", None, None),
        P("block", None, "node"),
        P("block", None, "node"),
        P("node"),
    )
    out_specs = (P("node", None), P("block", "node", None))
    return jax.shard_map(shards, mesh=mesh, in_specs=in_specs, out_specs=out_specs, check_vma=False)
```

```python
import functools
import jax
import jax.numpy as jnp
from jax import lax
from jax.experimental import pallas as pl
from jax.experimental.pallas import tpu as pltpu
from jax.sharding import PartitionSpec as P


CHUNKS = 2
F32 = jnp.float32
BF16 = jnp.bfloat16
PARAMS = pltpu.CompilerParams(vmem_limit_bytes=67043328)
ROW_PARAMS = pltpu.CompilerParams(vmem_limit_bytes=96 << 19)
WEIGH_PARAMS = pltpu.CompilerParams(vmem_limit_bytes=112 << 19)
SUM_PARAMS = pltpu.CompilerParams(vmem_limit_bytes=48 << 20)


def split(value):
    high = value.astype(jnp.bfloat16)
    low = (value - high.astype(F32)).astype(jnp.bfloat16)
    return high, low


def pair_of(j, bit):
    first = ((j >> bit) << (bit + 1)) + (j & ((1 << bit) - 1))
    return first, first + (1 << bit)


PARTS = 4


def rows_of(c, span):
    return slice(c * span, (c + 1) * span)


def take(ref, spans, span):
    return jnp.concatenate([ref[rows_of(c, span), :] for c in spans], axis=0)


def put(ref, spans, span, value):
    for n, c in enumerate(spans):
        ref[rows_of(c, span), :] = value[n * span : (n + 1) * span]


class Copies:
    def __init__(self, sems):
        self.sems, self.used = sems, 0

    def start(self, source, target):
        copy = pltpu.make_async_copy(source, target, self.sems.at[self.used])
        self.used += 1
        copy.start()
        return copy


def wait_all(copies):
    for copy in copies:
        copy.wait()


def part_rows(rows, halves):
    size = rows // PARTS // halves
    return [[pl.ds(h * (rows // halves) + p * size, size) for h in range(halves)] for p in range(PARTS)]


def pair_product(f_high, f_low, x):
    lhs = jnp.concatenate([f_high, f_low], axis=0)
    lhs = jnp.concatenate([lhs, lhs], axis=1)
    out = jnp.dot(lhs, jnp.concatenate(split(x), axis=0), preferred_element_type=F32)
    half = out.shape[0] // 2
    return out[:half] + out[half:]


def column_kernel(chunk, ranks, x_ref, f_ref, o_ref, x_buf, f_buf, buf_a, buf_b, o_buf, sems):
    levels, count, span = f_buf.shape[:3]
    rows, columns = x_buf.shape
    copies = Copies(sems)
    at = pl.ds(chunk * columns, columns)
    first = []
    size = count // PARTS
    for p in range(PARTS):
        first.append(
            [
                copies.start(f_ref.at[0, 0, pl.ds(p * size, size)], f_buf.at[0, pl.ds(p * size, size)]),
                copies.start(x_ref.at[pl.ds(p * size * span, size * span), at], x_buf.at[pl.ds(p * size * span, size * span)]),
            ]
        )
    later = [copies.start(f_ref.at[0, level], f_buf.at[level]) for level in range(1, levels)]
    bufs = [x_buf] + [(buf_a, buf_b)[level % 2] for level in range(levels - 1)] + [o_buf]
    row_ids = lax.broadcasted_iota(jnp.int32, (span, 2 * span), 0)
    outs = []
    for level in range(levels):
        if level:
            later[level - 1].wait()
        for p in range(PARTS):
            if level == 0:
                wait_all(first[p])
            for j in range(p * size // 2, (p + 1) * size // 2):
                pair = pair_of(j, level)
                factor = jnp.concatenate(
                    [jnp.where(row_ids < ranks[level, 0, c], f_buf[level, c], 0.0) for c in pair], axis=0
                )
                put(bufs[level + 1], pair, span, pair_product(*split(factor), take(bufs[level], pair, span)))
            if level == levels - 1:
                outs += [copies.start(o_buf.at[at], o_ref.at[at]) for at in part_rows(rows, 2)[p]]
    wait_all(outs)


def column_tree(x, factors, ranks, columns, chunk):
    rows = x.shape[0]
    return pl.pallas_call(
        functools.partial(column_kernel, chunk),
        out_shape=jax.ShapeDtypeStruct((rows, columns), F32),
        in_specs=[SMEM0, HBM, HBM],
        out_specs=HBM,
        scratch_shapes=[pltpu.VMEM((rows, columns), F32), pltpu.VMEM(factors.shape[1:], F32)]
        + [pltpu.VMEM((rows, columns), F32)] * 3
        + [pltpu.SemaphoreType.DMA((32,))],
        compiler_params=PARAMS,
        cost_estimate=pl.CostEstimate(flops=5 * 10**9, transcendentals=0, bytes_accessed=9 << 20),
        name="column_tree",
    )(ranks, x, factors)


SMEM0 = pl.BlockSpec(memory_space=pltpu.SMEM)
HBM = pl.BlockSpec(memory_space=pltpu.HBM)
ANYWHERE = pl.BlockSpec(memory_space=pl.ANY)
VMEM = pl.BlockSpec(memory_space=pltpu.VMEM)
SMEM = SMEM0


def quad_of(j, bit):
    base = ((j >> bit) << (bit + 2)) + (j & ((1 << bit) - 1))
    return [base + (n << bit) for n in range(4)]


def three(high, low, axis):
    return jnp.concatenate([high, high, low] if axis == 1 else [high, low, high], axis=axis)


def merge_kernel(first_bit, ranks, fa_ref, fb_ref, *refs):
    g_ref, t_ref = refs[-2:]
    span = fa_ref.shape[-2]
    lane = lax.broadcasted_iota(jnp.int32, (2 * span, 2 * span), 1)
    row_ids = lax.broadcasted_iota(jnp.int32, (span, 2 * span), 0)
    for s in range(2):

        @pl.when(pl.program_id(0) == s)
        def _(s=s):
            bit = first_bit + 2 * s
            masked = lambda ref, level, c: jnp.where(row_ids < ranks[level, 0, c], ref[0, c], 0.0)

            def body(j, carry):
                quad = quad_of(j, bit)
                rows = [None] * 4
                for a in range(2):
                    spans = (quad[a], quad[2 + a])
                    inner = jnp.concatenate([masked(fa_ref, 2 * s, c) for c in spans], axis=0)
                    outer = jnp.concatenate([masked(fb_ref, 2 * s + 1, c) for c in spans], axis=0)
                    outer = jnp.concatenate([jnp.where(lane < span, outer, 0.0), jnp.where(lane < span, 0.0, outer)], axis=0)
                    both = jnp.dot(three(*split(outer), 1), three(*split(inner), 0), preferred_element_type=F32)
                    both = jnp.concatenate([both[: 2 * span], both[2 * span :]], axis=1)
                    rows[a], rows[2 + a] = both[:span], both[span:]
                merged = jnp.concatenate(rows, axis=0)
                for out, value in ((g_ref, merged), (t_ref, merged.T)):
                    high, low = split(value)
                    out[0, j, 0] = high
                    out[0, j, 1] = low
                return carry

            lax.fori_loop(0, g_ref.shape[1], body, 0, unroll=4)


def merge_columns_kernel(first_bit, last, ranks, fa_ref, fb_ref, fe_ref, w_ref, v_ref, g_ref, t_ref):
    span = fa_ref.shape[-2]
    row_ids = lax.broadcasted_iota(jnp.int32, (span, 2 * span), 0)

    @pl.when(pl.program_id(0) == 0)
    def _():
        for j in range(w_ref.shape[0]):
            pair = pair_of(j, last)
            factor = jnp.concatenate([jnp.where(row_ids < ranks[last, 0, c], fe_ref[0, c], 0.0) for c in pair], axis=0)
            w_ref[j] = jnp.concatenate(split(factor), axis=0)
            v_ref[j] = jnp.concatenate(split(factor.T), axis=0)

    merge_kernel(first_bit, ranks, fa_ref, fb_ref, g_ref, t_ref)


def merge_rows_kernel(first_bit, ranks, fa_ref, fb_ref, weight_ref, b_ref, g_ref, t_ref):
    @pl.when(pl.program_id(0) == 0)
    def _():
        size = weight_ref.shape[1]
        for n in range(weight_ref.shape[0]):
            b_ref[n * size : (n + 1) * size, :] = jnp.broadcast_to(weight_ref[n : n + 1, :], (size, size)).T

    merge_kernel(first_bit, ranks, fa_ref, fb_ref, g_ref, t_ref)


def level_spec(factors, index):
    return pl.BlockSpec((None, 1) + factors.shape[2:], lambda s: (0, index(s), 0, 0, 0))


def merged_shapes(factors):
    quads, side = factors.shape[2] // 4, 4 * factors.shape[3]
    shape = jax.ShapeDtypeStruct((2, quads, 2, side, side), BF16)
    return shape, pl.BlockSpec((1, quads, 2, side, side), lambda s: (s, 0, 0, 0, 0))


def merge_columns(factors, ranks):
    shape, spec = merged_shapes(factors)
    last = factors.shape[1] - 1
    pairs, width = factors.shape[2] // 2, 2 * factors.shape[3]
    single = jax.ShapeDtypeStruct((pairs, 2 * width, width), BF16)
    single_spec = pl.BlockSpec(single.shape, lambda s: (0, 0, 0))
    return pl.pallas_call(
        functools.partial(merge_columns_kernel, 0, last),
        grid=(2,),
        out_shape=(single, single, shape, shape),
        in_specs=[SMEM]
        + [level_spec(factors, f) for f in (lambda s: 2 * s, lambda s: 2 * s + 1, lambda s: last)],
        out_specs=(single_spec, single_spec, spec, spec),
        compiler_params=PARAMS,
        cost_estimate=pl.CostEstimate(flops=10**10, transcendentals=0, bytes_accessed=15 << 20),
        name="merge_columns",
    )(ranks, factors, factors, factors)


def merge_rows(factors, ranks, weights, first_bit):
    shape, spec = merged_shapes(factors)
    weights = weights.reshape(-1, 128)
    rows = weights.size
    return pl.pallas_call(
        functools.partial(merge_rows_kernel, first_bit),
        grid=(2,),
        out_shape=(jax.ShapeDtypeStruct((rows, 128), F32), shape, shape),
        in_specs=[SMEM] + [level_spec(factors, f) for f in (lambda s: 2 * s, lambda s: 2 * s + 1)] + [whole2(weights.shape)],
        out_specs=(whole2((rows, 128)), spec, spec),
        compiler_params=PARAMS,
        cost_estimate=pl.CostEstimate(flops=10**10, transcendentals=0, bytes_accessed=12 << 20),
        name="merge_rows",
    )(ranks, factors, factors, weights)


def whole2(shape):
    return pl.BlockSpec(shape, lambda s: (0, 0))


def quad_product(g_ref, x):
    return jnp.dot(three(g_ref[0], g_ref[1], 1), three(*split(x), 0), preferred_element_type=F32)


def start_merged(copies, g_ref, g_buf, stage):
    size = g_buf.shape[1] // PARTS
    return [copies.start(g_ref.at[stage, pl.ds(p * size, size)], g_buf.at[stage, pl.ds(p * size, size)]) for p in range(PARTS)]


def quad_stage(g_buf, stage, bit, load, store, ready, done=None):
    size = g_buf.shape[1] // PARTS
    for p in range(PARTS):
        ready(p)
        for j in range(p * size, (p + 1) * size):
            quad = quad_of(j, bit)
            store(quad, quad_product(g_buf.at[stage, j], load(quad)))
        if done:
            done(p)


def merged_column_kernel(back, chunk, x_ref, w_ref, g_ref, *rest):
    o_ref, x_buf, w_buf, g_buf, buf_a, buf_b, o_buf, sems = rest[-8:]
    span = w_buf.shape[-1] // 2
    rows, columns = x_buf.shape
    at = pl.ds(chunk * columns, columns)
    copies = Copies(sems)
    w_size = w_buf.shape[0] // PARTS
    start_single = lambda p: copies.start(w_ref.at[pl.ds(p * w_size, w_size)], w_buf.at[pl.ds(p * w_size, w_size)])
    run_in, run_out = part_rows(rows, 2 if back else 1), part_rows(rows, 1 if back else 2)
    get = lambda p: [copies.start(x_ref.at[r] if back else x_ref.at[r, at], x_buf.at[r]) for r in run_in[p]]
    outs = []

    def leave(p):
        for r in run_out[p]:
            outs.append(copies.start(o_buf.at[r], o_ref.at[r, at] if back else o_ref.at[r]))

    def pairs(source, target, ready, done):
        for p in range(PARTS):
            ready(p)
            for j in range(p * w_size, (p + 1) * w_size):
                pair = pair_of(j, 4)
                high, low = w_buf[j, : 2 * span], w_buf[j, 2 * span :]
                put(target, pair, span, pair_product(high, low, take(source, pair, span)))
            done(p)

    def quads(stage, bit, source, target, ready, done=None):
        quad_stage(
            g_buf, stage, bit,
            lambda quad: take(source, quad, span), lambda quad, value: put(target, quad, span, value), ready, done,
        )

    if back:
        entry = [get(p) + [start_single(p)] for p in range(PARTS)]
        g_copies = {stage: start_merged(copies, g_ref, g_buf, stage) for stage in (1, 0)}
        pairs(x_buf, buf_a, lambda p: wait_all(entry[p]), lambda p: None)
        quads(1, 2, buf_a, buf_b, lambda p: g_copies[1][p].wait())
        quads(0, 0, buf_b, o_buf, lambda p: g_copies[0][p].wait(), leave)
    else:
        size = g_buf.shape[1] // PARTS
        entry = []
        for p in range(PARTS):
            g_part = copies.start(g_ref.at[0, pl.ds(p * size, size)], g_buf.at[0, pl.ds(p * size, size)])
            entry.append(get(p) + [g_part])
        g_copies = start_merged(copies, g_ref, g_buf, 1)
        singles = [start_single(p) for p in range(PARTS)]
        quads(0, 0, x_buf, buf_a, lambda p: wait_all(entry[p]))
        quads(1, 2, buf_a, buf_b, lambda p: g_copies[p].wait())
        pairs(buf_b, o_buf, lambda p: singles[p].wait(), leave)
    wait_all(outs)


def merged_columns(x, single, merged, back, columns, chunk=0, into=None, total=None, after=()):
    rows = x.shape[0]
    extra = list(after) if into is None else [into] + list(after)
    return pl.pallas_call(
        functools.partial(merged_column_kernel, back, chunk),
        out_shape=jax.ShapeDtypeStruct((rows, total or columns), F32),
        in_specs=[HBM] * 3 + [pl.BlockSpec(memory_space=pl.ANY)] * len(extra),
        out_specs=HBM,
        scratch_shapes=[pltpu.VMEM((rows, columns), F32), pltpu.VMEM(single.shape, BF16), pltpu.VMEM(merged.shape, BF16)]
        + [pltpu.VMEM((rows, columns), F32)] * 3
        + [pltpu.SemaphoreType.DMA((32,))],
        input_output_aliases={} if into is None else {3: 0},
        compiler_params=PARAMS,
        cost_estimate=pl.CostEstimate(flops=4 * 10**9, transcendentals=0, bytes_accessed=9 << 20),
        name="column_back" if back else "column_tree_merged",
    )(x, single, merged, *extra)


def row_kernel(first_bit, span, place, x_ref, g_ref, keep_ref, send_ref, x_buf, g_buf, buf, sems):
    swap = place[1] == 1
    rows = x_buf.shape[0]
    copies = Copies(sems)
    size = g_buf.shape[1] // PARTS
    entry = []
    for p in range(PARTS):
        r = part_rows(rows, 1)[p][0]
        g_part = copies.start(g_ref.at[0, pl.ds(p * size, size)], g_buf.at[0, pl.ds(p * size, size)])
        entry.append([g_part, copies.start(x_ref.at[r], x_buf.at[r])])
    g_copies = start_merged(copies, g_ref, g_buf, 1)

    def store(quad, value):
        half = 2 * span
        low, high = value[:half], value[half:]
        put(keep_ref, quad[:2], span, jnp.where(swap, high, low))
        put(send_ref, quad[:2], span, jnp.where(swap, low, high))

    load = lambda ref: lambda quad: take(ref, quad, span)
    quad_stage(
        g_buf, 0, first_bit, load(x_buf), lambda quad, value: put(buf, quad, span, value), lambda p: wait_all(entry[p])
    )
    quad_stage(g_buf, 1, first_bit + 2, load(buf), store, lambda p: g_copies[p].wait())


def row_tree(x, merged, place, first_bit, span):
    rows, columns = x.shape
    half = jax.ShapeDtypeStruct((rows // 2, columns), F32)
    return pl.pallas_call(
        functools.partial(row_kernel, first_bit, span),
        out_shape=(half, half),
        in_specs=[SMEM0, HBM, HBM],
        out_specs=(VMEM, VMEM),
        scratch_shapes=[pltpu.VMEM((rows, columns), F32), pltpu.VMEM(merged.shape, BF16), pltpu.VMEM((rows, columns), F32)]
        + [pltpu.SemaphoreType.DMA((32,))],
        compiler_params=ROW_PARAMS,
        cost_estimate=pl.CostEstimate(flops=3 * 10**9, transcendentals=0, bytes_accessed=8 << 20),
        name="row_tree",
    )(place, x, merged)


def add_halves_kernel(ring, place, keep_ref, got_ref, *outs):
    size = outs[0].shape[0]
    for d, out in enumerate(outs):
        rows = pl.ds(pl.multiple_of(lax.rem(place[0] + d, ring) * size, size), size)
        out[...] = keep_ref[rows, :] + got_ref[rows, :]


def add_halves(keep, got, place, ring):
    rows, columns = keep.shape
    size = rows // ring
    piece = jax.ShapeDtypeStruct((size, columns), F32)
    return pl.pallas_call(
        functools.partial(add_halves_kernel, ring),
        out_shape=(piece,) * ring,
        in_specs=[SMEM0, VMEM, VMEM],
        out_specs=(VMEM,) * ring,
        compiler_params=SUM_PARAMS,
        cost_estimate=pl.CostEstimate(flops=keep.size, transcendentals=0, bytes_accessed=12 * keep.size),
        name="add_halves",
    )(place, keep, got)


def add_pieces_kernel(*refs):
    total = refs[0][...]
    for ref in refs[1:-1]:
        total = total + ref[...]
    refs[-1][...] = total


def add_pieces(pieces):
    rows, columns = pieces[0].shape
    count = len(pieces)
    return pl.pallas_call(
        add_pieces_kernel,
        out_shape=jax.ShapeDtypeStruct((rows, columns), F32),
        in_specs=[VMEM] * count,
        out_specs=VMEM,
        compiler_params=SUM_PARAMS,
        cost_estimate=pl.CostEstimate(flops=4 * pieces[0].size, transcendentals=0, bytes_accessed=20 * pieces[0].size),
        name="add_pieces",
    )(*pieces)


def weigh_kernel(first_bit, span, ring, chunk, place, *refs):
    pieces = refs[: 2 * ring]
    w_ref, g_ref = refs[2 * ring : 2 * ring + 2]
    b_ref, o_ref, x_buf, w_buf, g_buf, buf, o_buf, sems = refs[-8:]
    size, columns = pieces[0].shape
    rows = x_buf.shape[0]
    copies = Copies(sems)
    entry, outs = [], []
    for n, piece in enumerate(pieces):
        side, d = divmod(n, ring)
        half = place[1] if side == 0 else 1 - place[1]
        begin = half * (ring * size) + lax.rem(place[0] + ring - d, ring) * size
        entry.append(copies.start(piece, x_buf.at[pl.ds(pl.multiple_of(begin, size), size)]))
    entry.append(copies.start(w_ref, w_buf))
    g_copies = {stage: start_merged(copies, g_ref, g_buf, stage) for stage in (1, 0)}
    wait_all(entry)
    block_out = copies.start(x_buf, b_ref.at[:, pl.ds(chunk * columns, columns)])

    def weighted(quad):
        value, weight = take(x_buf, quad, span), take(w_buf, quad, span)
        return value * jnp.concatenate([weight] * (columns // weight.shape[1]), axis=1)

    def leave(p):
        r = part_rows(rows, 1)[p][0]
        outs.append(copies.start(o_buf.at[r], o_ref.at[r]))

    quad_stage(
        g_buf, 1, first_bit + 2, weighted, lambda quad, value: put(buf, quad, span, value), lambda p: g_copies[1][p].wait()
    )
    quad_stage(
        g_buf, 0, first_bit, lambda quad: take(buf, quad, span),
        lambda quad, value: put(o_buf, quad, span, value), lambda p: g_copies[0][p].wait(), leave,
    )
    wait_all(outs + [block_out])


def weigh_back(pieces, weights, merged, place, first_bit, span, into, chunk, total):
    ring = len(pieces) // 2
    size, columns = pieces[0].shape
    rows = 2 * ring * size
    extra = [] if into is None else [into]
    return pl.pallas_call(
        functools.partial(weigh_kernel, first_bit, span, ring, chunk),
        out_shape=(jax.ShapeDtypeStruct((rows, total), F32), jax.ShapeDtypeStruct((rows, columns), F32)),
        in_specs=[SMEM0] + [ANYWHERE] * len(pieces) + [HBM] * (2 + len(extra)),
        out_specs=(HBM, HBM),
        scratch_shapes=[pltpu.VMEM((rows, columns), F32), pltpu.VMEM(weights.shape, F32), pltpu.VMEM(merged.shape, BF16)]
        + [pltpu.VMEM((rows, columns), F32)] * 2
        + [pltpu.SemaphoreType.DMA((32,))],
        input_output_aliases={3 + len(pieces): 0} if extra else {},
        compiler_params=WEIGH_PARAMS,
        cost_estimate=pl.CostEstimate(flops=3 * 10**9, transcendentals=0, bytes_accessed=12 << 20),
        name="weigh_back",
    )(place, *pieces, weights, merged, *extra)


def exchange(x):
    nodes = lax.axis_size("node")
    rows, columns = x.shape
    out = lax.all_to_all(x.reshape(nodes, rows // nodes, columns), "node", split_axis=0, concat_axis=0, tiled=True)
    return out.reshape(rows, columns)


def shards(vectors, col_factors, row_factors, col_ranks, row_ranks, row_weights):
    rows, total = vectors.shape[1:]
    columns = total // CHUNKS
    low_bits = col_factors.shape[1] - row_factors.shape[1]
    ring = lax.axis_size("block") // 2
    sibling = [(b, b ^ 1) for b in range(2 * ring)]
    shift = [[(b, (b + 2 * d) % (2 * ring)) for b in range(2 * ring)] for d in range(ring)]
    index = lax.axis_index("block")
    place = jnp.stack([index // 2, index % 2]).astype(jnp.int32)
    span = col_factors.shape[3]
    flat = vectors.reshape(rows, total)
    col_ranks = jnp.transpose(col_ranks, (1, 0, 2))
    row_ranks = jnp.transpose(row_ranks, (1, 0, 2))
    chunks = range(CHUNKS)
    t = column_tree(flat, col_factors, col_ranks, columns, 0)
    sent = [exchange(t)]
    single, single_back, col_merged, col_back = merge_columns(col_factors, col_ranks)
    weights, row_merged, row_back = merge_rows(row_factors, row_ranks, row_weights, low_bits)
    for n in chunks[1:]:
        t = merged_columns(flat, single, col_merged, False, columns, n, after=[weights])
        sent.append(exchange(t))
    halves = []
    for n in chunks:
        halves.append(row_tree(sent[n], row_merged, place, low_bits, span))

    def start(n):
        got = lax.ppermute(halves[n][1], "block", sibling)
        return add_halves(halves[n][0], got, place, ring)

    block_row = result = None
    back = []
    pieces = start(0)
    for n in chunks:
        later = n + 1 < CHUNKS
        got = [pieces[0]]
        for d in range(1, ring):
            got.append(lax.ppermute(pieces[d], "block", shift[d]))
        total_piece = add_pieces(got)
        mine = [total_piece]
        for d in range(1, ring):
            mine.append(lax.ppermute(total_piece, "block", shift[d]))
        if later:
            pieces = start(n + 1)
            mine[1:], pieces = lax.optimization_barrier((mine[1:], pieces))
        theirs = [lax.ppermute(piece, "block", sibling) for piece in mine]
        block_row, t = weigh_back(mine + theirs, weights, row_back, place, low_bits, span, block_row, n, total)
        back.append(exchange(t))
    for n in chunks:
        result = merged_columns(back[n], single_back, col_back, True, columns, n, result, total)
    return block_row, result.reshape(1, rows, total)


def solution(mesh):
    in_specs = (
        P("block", "node", None),
        P("block", None, "node", None, None),
        P("block", None, "node", None, None),
        P("block", None, "node"),
        P("block", None, "node"),
        P("node"),
    )
    out_specs = (P("node", None), P("block", "node", None))
    return jax.shard_map(shards, mesh=mesh, in_specs=in_specs, out_specs=out_specs, check_vma=False)
```
